512 devices in a mesh: dp: 4 (over x), expert: 16 (over z, core), etp: 8 (over y).
Axes of the slice: x: 4, y: 8, z: 8, core: 2. Of those that a mesh axis runs over, the one named last changes fastest.
Arguments:
- tokens: bfloat16 [9728, 4096], P(('dp', 'expert'), 'etp'), may hold values from -6 to 6
- cotangent: bfloat16 [9728, 4096], P(('dp', 'expert'), 'etp'), may hold values from -6 to 6
- gates: bfloat16 [9728, 8], P(('dp', 'expert')), may hold values from 0.049804688 to 0.5
- experts_hit: int32 [9728, 8], P(('dp', 'expert')), may hold values from -1 to 15, as said below
- positions: int32 [9728, 8], P(('dp', 'expert')), may hold values from -1 to 18, as said below
- gate_w: bfloat16 [16, 4096, 1536], P('expert', 'dp', 'etp'), may hold values from -0.09375 to 0.09375
- up_w: bfloat16 [16, 4096, 1536], P('expert', 'dp', 'etp'), may hold values from -0.09375 to 0.09375
- down_w: bfloat16 [16, 1536, 4096], P('expert', 'etp', 'dp'), may hold values from -0.15625 to 0.15625
Outputs:
- input_grad: bfloat16 [9728, 4096], P(('dp', 'expert'), 'etp')
- down_grad: bfloat16 [16, 1536, 4096], P('expert', 'etp', 'dp')
The draws below stay inside these ranges and needn't reach their ends.
Inputs may be any that keep to these rules, and one draw needn't show every extreme that they name: experts_hit and positions are -1 together, for routes to experts outside these 16. In the rows of one device, the routes to one expert hold positions 0 to n - 1 once each, with n between 1 and 19; no token names an expert twice. `positions`: see experts_hit.
All inputs are finite; a program needn't handle non-finite values.
Results may differ from the reference program's by a relative error of at most 0.018.
Values may be sent and summed in bfloat16 or wider, within the bound.
No kernel may reach another device: no remote copies, remote signals or barrier semaphores. Data moves between devices by JAX's collectives and lax.ppermute only.
A program may use at most 64 MiB of HBM per device.

```python
import math
import jax
import jax.numpy as jnp
from jax import lax

D = 4096
FF = 1536
TOP = 8
TOK_DEV = 152
CAP = 19
WINDOW = 16
TOKENS = 9728
N_DP = 4
N_ETP = 8


def route_tables(key):
    blocks = TOKENS // TOK_DEV
    base = jax.random.fold_in(key, 11)
    keys = jax.random.split(base, 5)
    perm_keys = jax.random.split(keys[0], blocks)
    places = jax.vmap(lambda one: jax.random.permutation(one, TOK_DEV))(perm_keys).astype(jnp.int32)
    first = jax.random.randint(keys[1], (blocks, WINDOW), 1, CAP + 1, dtype=jnp.int32)
    second = jax.random.randint(keys[2], (blocks, WINDOW), 1, CAP + 1, dtype=jnp.int32)
    loads = jnp.minimum(first, second)
    hottest = jax.random.randint(keys[3], (blocks // WINDOW,), 0, WINDOW, dtype=jnp.int32)
    hot_block = jnp.repeat(hottest, WINDOW)
    expert_ids = jnp.arange(WINDOW, dtype=jnp.int32)
    loads = jnp.where(expert_ids[None, :] == hot_block[:, None], CAP, loads)
    starts = expert_ids * TOK_DEV // WINDOW
    offsets = (places[:, :, None] - starts[None, None, :]) % TOK_DEV
    member = offsets < loads[:, None, :]
    ranks = jnp.cumsum(member.astype(jnp.int32), axis=2) - 1
    shifts = jax.random.randint(keys[4], (blocks, TOK_DEV), 0, TOP, dtype=jnp.int32)
    expert_cols = []
    place_cols = []
    for route in range(TOP):
        wanted = (route - shifts) % TOP
        chosen = member & (ranks == wanted[:, :, None])
        present = jnp.any(chosen, axis=2)
        expert = jnp.sum(jnp.where(chosen, expert_ids[None, None, :], 0), axis=2)
        place = jnp.sum(jnp.where(chosen, offsets, 0), axis=2)
        expert_cols.append(jnp.where(present, expert, -1))
        place_cols.append(jnp.where(present, place, -1))
    experts_all = jnp.stack(expert_cols, axis=2).reshape(TOKENS, TOP).astype(jnp.int32)
    places_all = jnp.stack(place_cols, axis=2).reshape(TOKENS, TOP).astype(jnp.int32)
    return (experts_all, places_all)


def draw_experts_hit(key, part):
    return route_tables(key)[0]


def draw_positions(key, part):
    return route_tables(key)[1]


def levels(stream_key, extent, cuts, least, top_value):
    factor_of, own = 1.0, jax.random.fold_in(stream_key, 6)
    for dim, parts in cuts:
        steps = jnp.exp(jax.random.uniform(jax.random.fold_in(own, dim), (parts,), jnp.float32, least / len(cuts), top_value / len(cuts)))
        factor_of = factor_of * jnp.repeat(steps, extent[dim] // parts).reshape([-1 if axis == dim else 1 for axis in range(len(extent))])
    return factor_of


def centred(rng, dims, width, reach, shards=(), held_as=jnp.bfloat16):
    entries = jax.random.normal(rng, dims, jnp.float32) * width
    if len(shards) > 0:
        entries = levels(rng, dims, shards, -0.22, 0.18) * entries
    return jnp.clip(entries, min=-reach, max=reach).astype(held_as)


def setup_inputs(seed: int = 0) -> dict:
    splits = jax.random.split(jax.random.key(seed), 9)
    tokens = centred(splits[0], (TOKENS, D), 1.0, 6.0, ((0, 64), (1, 8)))
    cotangent = centred(splits[1], (TOKENS, D), 1.0, 6.0, ((0, 64), (1, 8)))
    gates = jnp.clip(jnp.exp(math.log(0.5) - 2.306499 * jax.random.uniform(splits[2], (TOKENS, TOP), jnp.float32) ** levels(splits[2], (TOKENS, TOP), ((0, 64),), -0.2, 0.2)), 0.049804688, 0.5).astype(jnp.bfloat16)
    experts_hit = draw_experts_hit(jax.random.fold_in(splits[8], 71), 0)
    positions = draw_positions(jax.random.fold_in(splits[8], 71), 0)
    gate_w = centred(splits[5], (WINDOW, D, FF), D ** -0.5, 0.09375, ((0, 16), (1, 4), (2, 8)))
    up_w = centred(splits[6], (WINDOW, D, FF), D ** -0.5, 0.09375, ((0, 16), (1, 4), (2, 8)))
    down_w = centred(splits[7], (WINDOW, FF, D), FF ** -0.5, 0.15625, ((0, 16), (1, 8), (2, 4)))
    return dict(tokens=tokens, cotangent=cotangent, gates=gates, experts_hit=experts_hit, positions=positions, gate_w=gate_w, up_w=up_w, down_w=down_w)


def round_trip(value):
    held = lax.optimization_barrier(value.astype(jnp.bfloat16))
    return held.astype(jnp.float32)


def reference(tokens, cotangent, gates, experts_hit, positions, gate_w, up_w, down_w):
    slot_rows = N_DP * WINDOW * CAP
    total = WINDOW * slot_rows
    token_ids = jnp.arange(TOKENS, dtype=jnp.int32)
    block = token_ids // TOK_DEV
    replica = block // WINDOW
    source = block % WINDOW
    valid = experts_hit >= 0
    flat = jnp.where(valid, ((experts_hit * N_DP + replica[:, None]) * WINDOW + source[:, None]) * CAP + positions, total).astype(jnp.int32)
    flat_all = flat.reshape(-1)
    owners = jnp.zeros((total + 1,), jnp.int32).at[flat_all].set(jnp.repeat(token_ids, TOP))[:total]
    filled = jnp.zeros((total + 1,), jnp.bool_).at[flat_all].set(True)[:total]
    slot_gate = jnp.zeros((total + 1,), jnp.bfloat16).at[flat_all].set(gates.reshape(-1))[:total]
    block_ff = FF // N_ETP
    per_rep = WINDOW * CAP

    def expert_step(pack):
        owner, live, gate_col, w_gate, w_up, w_down = pack
        feats = jnp.where(live[:, None], tokens[owner], jnp.zeros((), jnp.bfloat16))
        grads = jnp.where(live[:, None], cotangent[owner], jnp.zeros((), jnp.bfloat16))
        gate_pre = jnp.dot(feats, w_gate, preferred_element_type=jnp.float32)
        up_pre = jnp.dot(feats, w_up, preferred_element_type=jnp.float32)
        sig = jax.nn.sigmoid(gate_pre)
        act = gate_pre * sig
        hidden = act * up_pre
        hidden_b = hidden.astype(jnp.bfloat16)
        back = jnp.dot(grads, w_down.T, preferred_element_type=jnp.float32)
        gate_f = gate_col.astype(jnp.float32)[:, None]
        d_hidden = gate_f * back
        d_gate_b = (d_hidden * up_pre * sig * (1.0 + gate_pre * (1.0 - sig))).astype(jnp.bfloat16)
        d_up_b = (d_hidden * act).astype(jnp.bfloat16)
        d_rows = jnp.zeros((slot_rows, D), jnp.float32)
        for part in range(N_ETP):
            lo = part * block_ff
            piece = jnp.dot(d_gate_b[:, lo:lo + block_ff], w_gate[:, lo:lo + block_ff].T, preferred_element_type=jnp.float32)
            piece = piece + jnp.dot(d_up_b[:, lo:lo + block_ff], w_up[:, lo:lo + block_ff].T, preferred_element_type=jnp.float32)
            d_rows = d_rows + round_trip(piece)
        scaled = (gate_f * grads.astype(jnp.float32)).astype(jnp.bfloat16)
        d_down = jnp.zeros((FF, D), jnp.float32)
        for rep in range(N_DP):
            lo = rep * per_rep
            term = jnp.dot(hidden_b[lo:lo + per_rep].T, scaled[lo:lo + per_rep], preferred_element_type=jnp.float32)
            d_down = d_down + round_trip(term)
        return d_rows, d_down.astype(jnp.bfloat16)

    d_rows, down_grad = lax.map(expert_step, (owners.reshape(WINDOW, slot_rows), filled.reshape(WINDOW, slot_rows), slot_gate.reshape(WINDOW, slot_rows), gate_w, up_w, down_w))
    table = jnp.concatenate([d_rows.reshape(total, D), jnp.zeros((1, D), jnp.float32)], axis=0)
    input_grad = jnp.zeros((TOKENS, D), jnp.float32)
    for route in range(TOP):
        input_grad = input_grad + table[flat[:, route]]
    return input_grad.astype(jnp.bfloat16), down_grad
```

```python
import jax
import jax.numpy as jnp
from jax import lax
from jax.sharding import PartitionSpec as P

CAP = 19


def expert_grads(feats, grads, gate_col, w_gate, w_up, w_down):
    gate_pre = jnp.dot(feats, w_gate, preferred_element_type=jnp.float32)
    up_pre = jnp.dot(feats, w_up, preferred_element_type=jnp.float32)
    sig = jax.nn.sigmoid(gate_pre)
    act = gate_pre * sig
    hidden_b = (act * up_pre).astype(jnp.bfloat16)
    back = lax.dot_general(
        grads, w_down, (((1,), (1,)), ((), ())), preferred_element_type=jnp.float32
    )
    gate_f = gate_col.astype(jnp.float32)[:, None]
    d_hidden = gate_f * back
    d_gate_b = (d_hidden * up_pre * sig * (1.0 + gate_pre * (1.0 - sig))).astype(jnp.bfloat16)
    d_up_b = (d_hidden * act).astype(jnp.bfloat16)
    d_part = lax.dot_general(
        d_gate_b, w_gate, (((1,), (1,)), ((), ())), preferred_element_type=jnp.float32
    )
    d_part = d_part + lax.dot_general(
        d_up_b, w_up, (((1,), (1,)), ((), ())), preferred_element_type=jnp.float32
    )
    scaled = (gate_f * grads).astype(jnp.bfloat16)
    term = lax.dot_general(
        hidden_b, scaled, (((0,), (0,)), ((), ())), preferred_element_type=jnp.float32
    )
    return (d_part.astype(jnp.bfloat16), term)


def local(tokens, cotangent, gates, experts_hit, positions, gate_w, up_w, down_w):
    width = lax.axis_size("expert")
    rows_dev, routes = experts_hit.shape
    slots = width * CAP
    narrow = tokens.shape[1]
    valid = experts_hit >= 0
    flat = jnp.where(valid, experts_hit * CAP + positions, slots)
    slot_ids = jnp.arange(slots, dtype=jnp.int32)
    hit = flat[None, :, :] == slot_ids[:, None, None]
    onehot = jnp.any(hit, axis=2).astype(jnp.bfloat16)
    slot_gate = jnp.sum(
        jnp.where(hit, gates.astype(jnp.float32)[None, :, :], 0.0), axis=(1, 2)
    ).astype(jnp.bfloat16)
    both = jnp.concatenate([tokens, cotangent], axis=1)
    packed = jnp.dot(onehot, both, preferred_element_type=jnp.float32).astype(jnp.bfloat16)
    recv = lax.all_to_all(
        packed.reshape(width, CAP, 2 * narrow), "expert", split_axis=0, concat_axis=0, tiled=True
    )
    recv_gate = lax.all_to_all(
        slot_gate.reshape(width, CAP), "expert", split_axis=0, concat_axis=0, tiled=True
    )
    pair = recv.reshape(slots, 2, narrow).transpose(1, 0, 2)
    full = lax.all_gather(pair, "etp", axis=2, tiled=True)
    feats = full[0]
    grads = full[1]
    w_gate, w_up, w_down = (
        lax.all_gather(gate_w[0], "dp", axis=0, tiled=True),
        lax.all_gather(up_w[0], "dp", axis=0, tiled=True),
        lax.all_gather(down_w[0], "dp", axis=1, tiled=True),
    )
    d_part_b, term = expert_grads(feats, grads, recv_gate.reshape(slots), w_gate, w_up, w_down)
    down_grad = lax.psum_scatter(term.astype(jnp.bfloat16), "dp", scatter_dimension=1, tiled=True)[
        None
    ]
    summed = lax.psum_scatter(d_part_b, "etp", scatter_dimension=1, tiled=True)
    returned = lax.all_to_all(
        summed.reshape(width, CAP, narrow), "expert", split_axis=0, concat_axis=0, tiled=True
    ).reshape(slots, narrow)
    total = lax.dot_general(
        onehot, returned, (((0,), (0,)), ((), ())), preferred_element_type=jnp.float32
    )
    input_grad = total.astype(jnp.bfloat16)
    return (input_grad, down_grad)


def solution(mesh):
    placed = (
        P(("dp", "expert"), "etp"),
        P(("dp", "expert"), "etp"),
        P(("dp", "expert"), None),
        P(("dp", "expert"), None),
        P(("dp", "expert"), None),
        P("expert", "dp", "etp"),
        P("expert", "dp", "etp"),
        P("expert", "etp", "dp"),
    )
    return jax.shard_map(
        local,
        mesh=mesh,
        in_specs=placed,
        out_specs=(P(("dp", "expert"), "etp"), P("expert", "etp", "dp")),
        check_vma=False,
    )
```

```python
import jax
import jax.numpy as jnp
from jax import lax
from jax.sharding import PartitionSpec as P

CAP = 19


def expert_grads(feats, grads, gate_col, w_gate, w_up, w_down_t):
    gate_pre = jnp.dot(feats, w_gate, preferred_element_type=jnp.float32)
    up_pre = jnp.dot(feats, w_up, preferred_element_type=jnp.float32)
    sig = jax.nn.sigmoid(gate_pre)
    act = gate_pre * sig
    hidden_b = (act * up_pre).astype(jnp.bfloat16)
    back = jnp.dot(grads, w_down_t, preferred_element_type=jnp.float32)
    gate_f = gate_col.astype(jnp.float32)[:, None]
    d_hidden = gate_f * back
    d_gate_b = (d_hidden * up_pre * sig * (1.0 + gate_pre * (1.0 - sig))).astype(jnp.bfloat16)
    d_up_b = (d_hidden * act).astype(jnp.bfloat16)
    d_part = lax.dot_general(
        d_gate_b, w_gate, (((1,), (1,)), ((), ())), preferred_element_type=jnp.float32
    )
    d_part = d_part + lax.dot_general(
        d_up_b, w_up, (((1,), (1,)), ((), ())), preferred_element_type=jnp.float32
    )
    scaled = (gate_f * grads).astype(jnp.bfloat16)
    term = lax.dot_general(
        hidden_b, scaled, (((0,), (0,)), ((), ())), preferred_element_type=jnp.float32
    )
    return (d_part.astype(jnp.bfloat16), term)


def local(tokens, cotangent, gates, experts_hit, positions, gate_w, up_w, down_w):
    width = lax.axis_size("expert")
    split = lax.axis_size("etp")
    rows_dev, routes = experts_hit.shape
    slots = width * CAP
    narrow = tokens.shape[1]
    valid = experts_hit >= 0
    flat = jnp.where(valid, experts_hit * CAP + positions, slots)
    slot_ids = jnp.arange(slots, dtype=jnp.int32)
    hit = flat[None, :, :] == slot_ids[:, None, None]
    onehot = jnp.any(hit, axis=2).astype(jnp.bfloat16)
    slot_gate = jnp.sum(
        jnp.where(hit, gates.astype(jnp.float32)[None, :, :], 0.0), axis=(1, 2)
    ).astype(jnp.bfloat16)
    both = jnp.concatenate([tokens, cotangent], axis=1)
    packed = jnp.dot(onehot, both, preferred_element_type=jnp.float32).astype(jnp.bfloat16)
    gate_row = jnp.pad(slot_gate.reshape(width, 1, CAP), ((0, 0), (0, 0), (0, 2 * narrow - CAP)))
    block = jnp.concatenate([packed.reshape(width, CAP, 2 * narrow), gate_row], axis=1)
    send = jnp.broadcast_to(block[:, None], (width, split, CAP + 1, 2 * narrow))
    recv = lax.all_to_all(
        send.reshape(width * split, CAP + 1, 2 * narrow),
        ("expert", "etp"),
        split_axis=0,
        concat_axis=0,
        tiled=True,
    ).reshape(width, split, CAP + 1, 2 * narrow)
    rows = recv[:, :, :CAP, :].transpose(0, 2, 1, 3)
    feats = rows[:, :, :, :narrow].reshape(slots, split * narrow)
    grads = rows[:, :, :, narrow:].reshape(slots, split * narrow)
    recv_gate = recv[:, 0, CAP, :CAP].reshape(slots)
    stack = jnp.stack([gate_w[0], up_w[0], down_w[0].T], axis=0)
    w_all = lax.all_gather(stack, "dp", axis=1, tiled=True)
    w_gate, w_up, w_down_t = w_all[0], w_all[1], w_all[2]
    d_part_b, term = expert_grads(feats, grads, recv_gate, w_gate, w_up, w_down_t)
    down_grad = lax.psum_scatter(term.astype(jnp.bfloat16), "dp", scatter_dimension=1, tiled=True)[
        None
    ]
    summed = lax.psum_scatter(d_part_b, "etp", scatter_dimension=1, tiled=True)
    returned = lax.all_to_all(
        summed.reshape(width, CAP, narrow), "expert", split_axis=0, concat_axis=0, tiled=True
    ).reshape(slots, narrow)
    total = lax.dot_general(
        onehot, returned, (((0,), (0,)), ((), ())), preferred_element_type=jnp.float32
    )
    input_grad = total.astype(jnp.bfloat16)
    return (input_grad, down_grad)


def solution(mesh):
    placed = (
        P(("dp", "expert"), "etp"),
        P(("dp", "expert"), "etp"),
        P(("dp", "expert"), None),
        P(("dp", "expert"), None),
        P(("dp", "expert"), None),
        P("expert", "dp", "etp"),
        P("expert", "dp", "etp"),
        P("expert", "etp", "dp"),
    )
    return jax.shard_map(
        local,
        mesh=mesh,
        in_specs=placed,
        out_specs=(P(("dp", "expert"), "etp"), P("expert", "etp", "dp")),
        check_vma=False,
    )
```

```python
import jax
import jax.numpy as jnp
from jax import lax
from jax.sharding import PartitionSpec as P

CAP = 19


def expert_grads(feats, grads, gate_col, w_gate, w_up, w_down_t):
    gate_pre = jnp.dot(feats, w_gate, preferred_element_type=jnp.float32)
    up_pre = jnp.dot(feats, w_up, preferred_element_type=jnp.float32)
    sig = jax.nn.sigmoid(gate_pre)
    act = gate_pre * sig
    hidden_b = (act * up_pre).astype(jnp.bfloat16)
    back = jnp.dot(grads, w_down_t, preferred_element_type=jnp.float32)
    gate_f = gate_col.astype(jnp.float32)[:, None]
    d_hidden = gate_f * back
    d_gate_b = (d_hidden * up_pre * sig * (1.0 + gate_pre * (1.0 - sig))).astype(jnp.bfloat16)
    d_up_b = (d_hidden * act).astype(jnp.bfloat16)
    d_part = lax.dot_general(
        d_gate_b, w_gate, (((1,), (1,)), ((), ())), preferred_element_type=jnp.float32
    )
    d_part = d_part + lax.dot_general(
        d_up_b, w_up, (((1,), (1,)), ((), ())), preferred_element_type=jnp.float32
    )
    scaled = (gate_f * grads).astype(jnp.bfloat16)
    term = lax.dot_general(
        hidden_b, scaled, (((0,), (0,)), ((), ())), preferred_element_type=jnp.float32
    )
    return (d_part.astype(jnp.bfloat16), term)


def gather_dp(piece, axis):
    size = lax.axis_size("dp")
    me = lax.axis_index("dp")
    got = [piece]
    for shift in range(1, size):
        got.append(lax.ppermute(piece, "dp", [(i, (i + shift) % size) for i in range(size)]))
    order = (me - jnp.arange(size, dtype=jnp.int32)) % size
    ranked = jnp.take(jnp.stack(got, axis=0), order, axis=0)
    return jnp.concatenate([ranked[i] for i in range(size)], axis=axis)


def scatter_sum_dp(term_b):
    size = lax.axis_size("dp")
    me = lax.axis_index("dp")
    quarter = term_b.shape[1] // size
    parts = term_b.reshape(term_b.shape[0], size, quarter)
    total = jnp.take(parts, me, axis=1).astype(jnp.float32)
    for shift in range(1, size):
        outgoing = jnp.take(parts, (me + shift) % size, axis=1)
        total = total + lax.ppermute(
            outgoing, "dp", [(i, (i + shift) % size) for i in range(size)]
        ).astype(jnp.float32)
    return total.astype(jnp.bfloat16)


def local(tokens, cotangent, gates, experts_hit, positions, gate_w, up_w, down_w):
    width = lax.axis_size("expert")
    rows_dev, routes = experts_hit.shape
    slots = width * CAP
    narrow = tokens.shape[1]
    valid = experts_hit >= 0
    flat = jnp.where(valid, experts_hit * CAP + positions, slots)
    slot_ids = jnp.arange(slots, dtype=jnp.int32)
    hit = flat[None, :, :] == slot_ids[:, None, None]
    onehot = jnp.any(hit, axis=2).astype(jnp.bfloat16)
    slot_gate = jnp.sum(
        jnp.where(hit, gates.astype(jnp.float32)[None, :, :], 0.0), axis=(1, 2)
    ).astype(jnp.bfloat16)
    both = jnp.concatenate([tokens, cotangent], axis=1)
    packed = jnp.dot(onehot, both, preferred_element_type=jnp.float32).astype(jnp.bfloat16)
    gate_row = jnp.pad(slot_gate.reshape(width, 1, CAP), ((0, 0), (0, 0), (0, 2 * narrow - CAP)))
    block = jnp.concatenate([packed.reshape(width, CAP, 2 * narrow), gate_row], axis=1)
    recv = lax.all_to_all(block, "expert", split_axis=0, concat_axis=0, tiled=True)
    recv_gate = recv[:, CAP, :CAP].reshape(slots)
    pair = recv[:, :CAP, :].reshape(slots, 2, narrow).transpose(1, 0, 2)
    full = lax.all_gather(pair, "etp", axis=2, tiled=True)
    feats = full[0]
    grads = full[1]
    stack = jnp.stack([gate_w[0], up_w[0], down_w[0].T], axis=0)
    w_all = gather_dp(stack, 1)
    w_gate, w_up, w_down_t = w_all[0], w_all[1], w_all[2]
    d_part_b, term = expert_grads(feats, grads, recv_gate, w_gate, w_up, w_down_t)
    down_grad = scatter_sum_dp(term.astype(jnp.bfloat16))[None]
    summed = lax.psum_scatter(d_part_b, "etp", scatter_dimension=1, tiled=True)
    returned = lax.all_to_all(
        summed.reshape(width, CAP, narrow), "expert", split_axis=0, concat_axis=0, tiled=True
    ).reshape(slots, narrow)
    total = lax.dot_general(
        onehot, returned, (((0,), (0,)), ((), ())), preferred_element_type=jnp.float32
    )
    input_grad = total.astype(jnp.bfloat16)
    return (input_grad, down_grad)


def solution(mesh):
    placed = (
        P(("dp", "expert"), "etp"),
        P(("dp", "expert"), "etp"),
        P(("dp", "expert"), None),
        P(("dp", "expert"), None),
        P(("dp", "expert"), None),
        P("expert", "dp", "etp"),
        P("expert", "dp", "etp"),
        P("expert", "etp", "dp"),
    )
    return jax.shard_map(
        local,
        mesh=mesh,
        in_specs=placed,
        out_specs=(P(("dp", "expert"), "etp"), P("expert", "etp", "dp")),
        check_vma=False,
    )
```

```python
import jax
import jax.numpy as jnp
from jax import lax
from jax.sharding import PartitionSpec as P

CAP = 19


def expert_grads(feats, grads, gate_col, w_gate, w_up, w_down_t):
    split, _, narrow = feats.shape
    by_block = (((0, 2), (0, 1)), ((), ()))
    gate_pre = lax.dot_general(
        feats, w_gate.reshape(split, narrow, -1), by_block, preferred_element_type=jnp.float32
    )
    up_pre = lax.dot_general(
        feats, w_up.reshape(split, narrow, -1), by_block, preferred_element_type=jnp.float32
    )
    sig = jax.nn.sigmoid(gate_pre)
    act = gate_pre * sig
    hidden_b = (act * up_pre).astype(jnp.bfloat16)
    back = lax.dot_general(
        grads, w_down_t.reshape(split, narrow, -1), by_block, preferred_element_type=jnp.float32
    )
    gate_f = gate_col.astype(jnp.float32)[:, None]
    d_hidden = gate_f * back
    d_gate_b = (d_hidden * up_pre * sig * (1.0 + gate_pre * (1.0 - sig))).astype(jnp.bfloat16)
    d_up_b = (d_hidden * act).astype(jnp.bfloat16)
    d_part = lax.dot_general(
        d_gate_b, w_gate, (((1,), (1,)), ((), ())), preferred_element_type=jnp.float32
    )
    d_part = d_part + lax.dot_general(
        d_up_b, w_up, (((1,), (1,)), ((), ())), preferred_element_type=jnp.float32
    )
    scaled = (gate_f[None] * grads).astype(jnp.bfloat16)
    term = lax.dot_general(
        hidden_b, scaled, (((0,), (1,)), ((), ())), preferred_element_type=jnp.float32
    )
    return (d_part.astype(jnp.bfloat16), term.reshape(term.shape[0], split * narrow))


def gather_dp(piece, axis):
    size = lax.axis_size("dp")
    me = lax.axis_index("dp")
    got = [piece]
    for shift in range(1, size):
        got.append(lax.ppermute(piece, "dp", [(i, (i + shift) % size) for i in range(size)]))
    order = (me - jnp.arange(size, dtype=jnp.int32)) % size
    ranked = jnp.take(jnp.stack(got, axis=0), order, axis=0)
    return jnp.concatenate([ranked[i] for i in range(size)], axis=axis)


def scatter_sum_dp(term_b):
    size = lax.axis_size("dp")
    me = lax.axis_index("dp")
    quarter = term_b.shape[1] // size
    parts = term_b.reshape(term_b.shape[0], size, quarter)
    total = jnp.take(parts, me, axis=1).astype(jnp.float32)
    for shift in range(1, size):
        outgoing = jnp.take(parts, (me + shift) % size, axis=1)
        total = total + lax.ppermute(
            outgoing, "dp", [(i, (i + shift) % size) for i in range(size)]
        ).astype(jnp.float32)
    return total.astype(jnp.bfloat16)


def local(tokens, cotangent, gates, experts_hit, positions, gate_w, up_w, down_w):
    width = lax.axis_size("expert")
    rows_dev, routes = experts_hit.shape
    slots = width * CAP
    narrow = tokens.shape[1]
    valid = experts_hit >= 0
    flat = jnp.where(valid, experts_hit * CAP + positions, slots)
    slot_ids = jnp.arange(slots, dtype=jnp.int32)
    hit = flat[None, :, :] == slot_ids[:, None, None]
    onehot = jnp.any(hit, axis=2).astype(jnp.bfloat16)
    slot_gate = jnp.sum(
        jnp.where(hit, gates.astype(jnp.float32)[None, :, :], 0.0), axis=(1, 2)
    ).astype(jnp.bfloat16)
    packed_x = jnp.dot(onehot, tokens, preferred_element_type=jnp.float32).astype(jnp.bfloat16)
    packed_dy = jnp.dot(onehot, cotangent, preferred_element_type=jnp.float32).astype(jnp.bfloat16)
    gate_row = jnp.pad(slot_gate.reshape(width, 1, CAP), ((0, 0), (0, 0), (0, narrow - CAP)))
    block = jnp.concatenate(
        [
            packed_x.reshape(width, CAP, narrow),
            gate_row,
            packed_dy.reshape(width, CAP, narrow),
            jnp.zeros_like(gate_row),
        ],
        axis=1,
    )
    recv = lax.all_to_all(block, "expert", split_axis=0, concat_axis=0, tiled=True)
    recv_gate = recv[:, CAP, :CAP].reshape(slots)
    pair = jnp.stack(
        [
            recv[:, :CAP, :].reshape(slots, narrow),
            recv[:, CAP + 1 : 2 * CAP + 1, :].reshape(slots, narrow),
        ],
        axis=0,
    )
    full = lax.all_gather(pair, "etp", axis=1, tiled=False)
    feats = full[0]
    grads = full[1]
    stack = jnp.stack([gate_w[0], up_w[0], down_w[0].T], axis=0)
    w_all = gather_dp(stack, 1)
    w_gate, w_up, w_down_t = w_all[0], w_all[1], w_all[2]
    d_part_b, term = expert_grads(feats, grads, recv_gate, w_gate, w_up, w_down_t)
    down_grad = scatter_sum_dp(term.astype(jnp.bfloat16))[None]
    summed = lax.psum_scatter(d_part_b, "etp", scatter_dimension=1, tiled=True)
    returned = lax.all_to_all(
        summed.reshape(width, CAP, narrow), "expert", split_axis=0, concat_axis=0, tiled=True
    ).reshape(slots, narrow)
    total = lax.dot_general(
        onehot, returned, (((0,), (0,)), ((), ())), preferred_element_type=jnp.float32
    )
    input_grad = total.astype(jnp.bfloat16)
    return (input_grad, down_grad)


def solution(mesh):
    placed = (
        P(("dp", "expert"), "etp"),
        P(("dp", "expert"), "etp"),
        P(("dp", "expert"), None),
        P(("dp", "expert"), None),
        P(("dp", "expert"), None),
        P("expert", "dp", "etp"),
        P("expert", "dp", "etp"),
        P("expert", "etp", "dp"),
    )
    return jax.shard_map(
        local,
        mesh=mesh,
        in_specs=placed,
        out_specs=(P(("dp", "expert"), "etp"), P("expert", "etp", "dp")),
        check_vma=False,
    )
```

```python
import jax
import jax.numpy as jnp
from jax import lax
from jax.sharding import PartitionSpec as P

CAP = 19


def expert_grads(feats, grads, gate_col, pieces):
    split, slots, narrow = feats.shape
    size = len(pieces)
    me = lax.axis_index("dp")
    per = split // size
    quarter = per * narrow
    by_block = (((0, 2), (0, 1)), ((), ()))
    gate_pre = 0.0
    up_pre = 0.0
    back = 0.0
    for k, piece in enumerate(pieces):
        start = ((me - k) % size) * per
        f_k = lax.dynamic_slice_in_dim(feats, start, per, axis=0)
        g_k = lax.dynamic_slice_in_dim(grads, start, per, axis=0)
        w_k = piece.reshape(3, per, narrow, -1)
        gate_pre = gate_pre + lax.dot_general(f_k, w_k[0], by_block, preferred_element_type=jnp.float32)
        up_pre = up_pre + lax.dot_general(f_k, w_k[1], by_block, preferred_element_type=jnp.float32)
        back = back + lax.dot_general(g_k, w_k[2], by_block, preferred_element_type=jnp.float32)
    sig = jax.nn.sigmoid(gate_pre)
    act = gate_pre * sig
    hidden_b = (act * up_pre).astype(jnp.bfloat16)
    gate_f = gate_col.astype(jnp.float32)[:, None]
    d_hidden = gate_f * back
    d_gate_b = (d_hidden * up_pre * sig * (1.0 + gate_pre * (1.0 - sig))).astype(jnp.bfloat16)
    d_up_b = (d_hidden * act).astype(jnp.bfloat16)
    d_part = jnp.zeros((slots, size * quarter), jnp.bfloat16)
    for k, piece in enumerate(pieces):
        part = lax.dot_general(
            d_gate_b, piece[0], (((1,), (1,)), ((), ())), preferred_element_type=jnp.float32
        )
        part = part + lax.dot_general(
            d_up_b, piece[1], (((1,), (1,)), ((), ())), preferred_element_type=jnp.float32
        )
        d_part = lax.dynamic_update_slice_in_dim(
            d_part, part.astype(jnp.bfloat16), ((me - k) % size) * quarter, axis=1
        )
    scaled = (gate_f[None] * grads).astype(jnp.bfloat16)
    term = lax.dot_general(
        hidden_b, scaled, (((0,), (1,)), ((), ())), preferred_element_type=jnp.float32
    )
    return (d_part, term.reshape(term.shape[0], split * narrow))


def pieces_dp(piece):
    size = lax.axis_size("dp")
    got = [piece]
    for shift in range(1, size):
        got.append(lax.ppermute(piece, "dp", [(i, (i + shift) % size) for i in range(size)]))
    return got


def scatter_sum_dp(term_b):
    size = lax.axis_size("dp")
    me = lax.axis_index("dp")
    quarter = term_b.shape[1] // size
    parts = term_b.reshape(term_b.shape[0], size, quarter)
    total = jnp.take(parts, me, axis=1).astype(jnp.float32)
    for shift in range(1, size):
        outgoing = jnp.take(parts, (me + shift) % size, axis=1)
        total = total + lax.ppermute(
            outgoing, "dp", [(i, (i + shift) % size) for i in range(size)]
        ).astype(jnp.float32)
    return total.astype(jnp.bfloat16)


def local(tokens, cotangent, gates, experts_hit, positions, gate_w, up_w, down_w):
    width = lax.axis_size("expert")
    rows_dev, routes = experts_hit.shape
    slots = width * CAP
    narrow = tokens.shape[1]
    valid = experts_hit >= 0
    flat = jnp.where(valid, experts_hit * CAP + positions, slots)
    slot_ids = jnp.arange(slots, dtype=jnp.int32)
    hit = flat[None, :, :] == slot_ids[:, None, None]
    onehot = jnp.any(hit, axis=2).astype(jnp.bfloat16)
    slot_gate = jnp.sum(
        jnp.where(hit, gates.astype(jnp.float32)[None, :, :], 0.0), axis=(1, 2)
    ).astype(jnp.bfloat16)
    packed_x = jnp.dot(onehot, tokens, preferred_element_type=jnp.float32).astype(jnp.bfloat16)
    packed_dy = jnp.dot(onehot, cotangent, preferred_element_type=jnp.float32).astype(jnp.bfloat16)
    gate_row = jnp.pad(slot_gate.reshape(width, 1, CAP), ((0, 0), (0, 0), (0, narrow - CAP)))
    block = jnp.concatenate(
        [
            packed_x.reshape(width, CAP, narrow),
            gate_row,
            packed_dy.reshape(width, CAP, narrow),
            jnp.zeros_like(gate_row),
        ],
        axis=1,
    )
    recv = lax.all_to_all(block, "expert", split_axis=0, concat_axis=0, tiled=True)
    recv_gate = recv[:, CAP, :CAP].reshape(slots)
    pair = jnp.stack(
        [
            recv[:, :CAP, :].reshape(slots, narrow),
            recv[:, CAP + 1 : 2 * CAP + 1, :].reshape(slots, narrow),
        ],
        axis=0,
    )
    full = lax.all_gather(pair, "etp", axis=1, tiled=False)
    feats = full[0]
    grads = full[1]
    stack = jnp.stack([gate_w[0], up_w[0], down_w[0].T], axis=0)
    d_part_b, term = expert_grads(feats, grads, recv_gate, pieces_dp(stack))
    down_grad = scatter_sum_dp(term.astype(jnp.bfloat16))[None]
    summed = lax.psum_scatter(d_part_b, "etp", scatter_dimension=1, tiled=True)
    returned = lax.all_to_all(
        summed.reshape(width, CAP, narrow), "expert", split_axis=0, concat_axis=0, tiled=True
    ).reshape(slots, narrow)
    total = lax.dot_general(
        onehot, returned, (((0,), (0,)), ((), ())), preferred_element_type=jnp.float32
    )
    input_grad = total.astype(jnp.bfloat16)
    return (input_grad, down_grad)


def solution(mesh):
    placed = (
        P(("dp", "expert"), "etp"),
        P(("dp", "expert"), "etp"),
        P(("dp", "expert"), None),
        P(("dp", "expert"), None),
        P(("dp", "expert"), None),
        P("expert", "dp", "etp"),
        P("expert", "dp", "etp"),
        P("expert", "etp", "dp"),
    )
    return jax.shard_map(
        local,
        mesh=mesh,
        in_specs=placed,
        out_specs=(P(("dp", "expert"), "etp"), P("expert", "etp", "dp")),
        check_vma=False,
    )
```

```python
import jax
import jax.numpy as jnp
from jax import lax
from jax.sharding import PartitionSpec as P

CAP = 19


def expert_grads(feats, grads, gate_col, pieces):
    slots = feats.shape[0]
    size = len(pieces)
    quarter = pieces[0].shape[1]
    me = lax.axis_index("dp")
    gate_pre = 0.0
    up_pre = 0.0
    back = 0.0
    for k, piece in enumerate(pieces):
        start = ((me - k) % size) * quarter
        f_k = lax.dynamic_slice_in_dim(feats, start, quarter, axis=1)
        g_k = lax.dynamic_slice_in_dim(grads, start, quarter, axis=1)
        gate_pre = gate_pre + jnp.dot(f_k, piece[0], preferred_element_type=jnp.float32)
        up_pre = up_pre + jnp.dot(f_k, piece[1], preferred_element_type=jnp.float32)
        back = back + jnp.dot(g_k, piece[2], preferred_element_type=jnp.float32)
    sig = jax.nn.sigmoid(gate_pre)
    act = gate_pre * sig
    hidden_b = (act * up_pre).astype(jnp.bfloat16)
    gate_f = gate_col.astype(jnp.float32)[:, None]
    d_hidden = gate_f * back
    d_gate_b = (d_hidden * up_pre * sig * (1.0 + gate_pre * (1.0 - sig))).astype(jnp.bfloat16)
    d_up_b = (d_hidden * act).astype(jnp.bfloat16)
    d_part = jnp.zeros((slots, size * quarter), jnp.bfloat16)
    for k, piece in enumerate(pieces):
        part = lax.dot_general(
            d_gate_b, piece[0], (((1,), (1,)), ((), ())), preferred_element_type=jnp.float32
        )
        part = part + lax.dot_general(
            d_up_b, piece[1], (((1,), (1,)), ((), ())), preferred_element_type=jnp.float32
        )
        d_part = lax.dynamic_update_slice_in_dim(
            d_part, part.astype(jnp.bfloat16), ((me - k) % size) * quarter, axis=1
        )
    scaled = (gate_f * grads).astype(jnp.bfloat16)
    term = lax.dot_general(
        hidden_b, scaled, (((0,), (0,)), ((), ())), preferred_element_type=jnp.float32
    )
    return (d_part, term)


def pieces_dp(piece):
    size = lax.axis_size("dp")
    got = [piece]
    for shift in range(1, size):
        got.append(lax.ppermute(piece, "dp", [(i, (i + shift) % size) for i in range(size)]))
    return got


def scatter_sum_dp(term_b):
    size = lax.axis_size("dp")
    me = lax.axis_index("dp")
    quarter = term_b.shape[1] // size
    parts = term_b.reshape(term_b.shape[0], size, quarter)
    total = jnp.take(parts, me, axis=1).astype(jnp.float32)
    for shift in range(1, size):
        outgoing = jnp.take(parts, (me + shift) % size, axis=1)
        total = total + lax.ppermute(
            outgoing, "dp", [(i, (i + shift) % size) for i in range(size)]
        ).astype(jnp.float32)
    return total.astype(jnp.bfloat16)


def local(tokens, cotangent, gates, experts_hit, positions, gate_w, up_w, down_w):
    width = lax.axis_size("expert")
    rows_dev, routes = experts_hit.shape
    slots = width * CAP
    narrow = tokens.shape[1]
    valid = experts_hit >= 0
    flat = jnp.where(valid, experts_hit * CAP + positions, slots)
    slot_ids = jnp.arange(slots, dtype=jnp.int32)
    hit = flat[None, :, :] == slot_ids[:, None, None]
    onehot = jnp.any(hit, axis=2).astype(jnp.bfloat16)
    slot_gate = jnp.sum(
        jnp.where(hit, gates.astype(jnp.float32)[None, :, :], 0.0), axis=(1, 2)
    ).astype(jnp.bfloat16)
    packed_x = jnp.dot(onehot, tokens, preferred_element_type=jnp.float32).astype(jnp.bfloat16)
    packed_dy = jnp.dot(onehot, cotangent, preferred_element_type=jnp.float32).astype(jnp.bfloat16)
    gate_row = jnp.pad(slot_gate.reshape(width, 1, CAP), ((0, 0), (0, 0), (0, narrow - CAP)))
    block = jnp.concatenate(
        [
            packed_x.reshape(width, CAP, narrow),
            gate_row,
            packed_dy.reshape(width, CAP, narrow),
            jnp.zeros_like(gate_row),
        ],
        axis=1,
    )
    recv = lax.all_to_all(block, "expert", split_axis=0, concat_axis=0, tiled=True)
    recv_gate = recv[:, CAP, :CAP].reshape(slots)
    pair = jnp.stack(
        [
            recv[:, :CAP, :].reshape(slots, narrow),
            recv[:, CAP + 1 : 2 * CAP + 1, :].reshape(slots, narrow),
        ],
        axis=0,
    )
    full = lax.all_gather(pair, "etp", axis=2, tiled=True)
    feats = full[0]
    grads = full[1]
    stack = jnp.stack([gate_w[0], up_w[0], down_w[0].T], axis=0)
    d_part_b, term = expert_grads(feats, grads, recv_gate, pieces_dp(stack))
    down_grad = scatter_sum_dp(term.astype(jnp.bfloat16))[None]
    summed = lax.psum_scatter(d_part_b, "etp", scatter_dimension=1, tiled=True)
    returned = lax.all_to_all(
        summed.reshape(width, CAP, narrow), "expert", split_axis=0, concat_axis=0, tiled=True
    ).reshape(slots, narrow)
    total = lax.dot_general(
        onehot, returned, (((0,), (0,)), ((), ())), preferred_element_type=jnp.float32
    )
    input_grad = total.astype(jnp.bfloat16)
    return (input_grad, down_grad)


def solution(mesh):
    placed = (
        P(("dp", "expert"), "etp"),
        P(("dp", "expert"), "etp"),
        P(("dp", "expert"), None),
        P(("dp", "expert"), None),
        P(("dp", "expert"), None),
        P("expert", "dp", "etp"),
        P("expert", "dp", "etp"),
        P("expert", "etp", "dp"),
    )
    return jax.shard_map(
        local,
        mesh=mesh,
        in_specs=placed,
        out_specs=(P(("dp", "expert"), "etp"), P("expert", "etp", "dp")),
        check_vma=False,
    )
```

```python
import jax
import jax.numpy as jnp
from jax import lax
from jax.experimental import pallas as pl
from jax.experimental.pallas import tpu as pltpu
from jax.sharding import PartitionSpec as P

CAP = 19


def _expert_kernel(me_ref, rows_ref, gate_ref, w0_ref, w1_ref, w2_ref, w3_ref, q_ref, term_ref):
    size = 4
    quarter = w0_ref.shape[1]
    me = me_ref[0]
    pieces = (w0_ref, w1_ref, w2_ref, w3_ref)
    gate_pre = None
    for k, w_ref in enumerate(pieces):
        start = pl.multiple_of(((me + size - k) % size) * quarter, quarter)
        f_k = rows_ref[0, :, pl.ds(start, quarter)]
        g_k = rows_ref[1, :, pl.ds(start, quarter)]
        a = jnp.dot(f_k, w_ref[0], preferred_element_type=jnp.float32)
        b = jnp.dot(f_k, w_ref[1], preferred_element_type=jnp.float32)
        c = jnp.dot(g_k, w_ref[2], preferred_element_type=jnp.float32)
        if gate_pre is None:
            gate_pre, up_pre, back = a, b, c
        else:
            gate_pre, up_pre, back = gate_pre + a, up_pre + b, back + c
    sig = jax.nn.sigmoid(gate_pre)
    act = gate_pre * sig
    hidden = act * up_pre
    gate_f = gate_ref[...].astype(jnp.float32)
    d_hidden = gate_f * back
    d_gate_b = (d_hidden * up_pre * sig * (1.0 + gate_pre * (1.0 - sig))).astype(jnp.bfloat16)
    d_up_b = (d_hidden * act).astype(jnp.bfloat16)
    nt = (((1,), (1,)), ((), ()))
    for k, w_ref in enumerate(pieces):
        start = pl.multiple_of(((me + size - k) % size) * quarter, quarter)
        part = lax.dot_general(d_gate_b, w_ref[0], nt, preferred_element_type=jnp.float32)
        part = part + lax.dot_general(d_up_b, w_ref[1], nt, preferred_element_type=jnp.float32)
        q_ref[:, pl.ds(start, quarter)] = part.astype(jnp.bfloat16)
    hidden_t = hidden.T.astype(jnp.bfloat16)
    scaled = (gate_f * rows_ref[1].astype(jnp.float32)).astype(jnp.bfloat16)
    term_ref[...] = jnp.dot(hidden_t, scaled, preferred_element_type=jnp.float32).astype(jnp.bfloat16)


def expert_kernel(me, rows, gate_col, pieces):
    _, slots, width = rows.shape
    ffb = pieces[0].shape[2]
    vmem = pltpu.VMEM
    return pl.pallas_call(
        _expert_kernel,
        out_shape=(
            jax.ShapeDtypeStruct((slots, width), jnp.bfloat16),
            jax.ShapeDtypeStruct((ffb, width), jnp.bfloat16),
        ),
        in_specs=[pl.BlockSpec(memory_space=pltpu.SMEM)] + [pl.BlockSpec(memory_space=vmem)] * 6,
        out_specs=(pl.BlockSpec(memory_space=vmem), pl.BlockSpec(memory_space=vmem)),
        compiler_params=pltpu.CompilerParams(vmem_limit_bytes=48 * 1024 * 1024),
    )(me.reshape(1), rows, gate_col.reshape(slots, 1), *pieces)


def pieces_dp(piece):
    size = lax.axis_size("dp")
    got = [piece]
    for shift in range(1, size):
        got.append(lax.ppermute(piece, "dp", [(i, (i + shift) % size) for i in range(size)]))
    return got


def scatter_sum_dp(term_b):
    size = lax.axis_size("dp")
    me = lax.axis_index("dp")
    quarter = term_b.shape[1] // size
    parts = term_b.reshape(term_b.shape[0], size, quarter)
    total = jnp.take(parts, me, axis=1).astype(jnp.float32)
    for shift in range(1, size):
        outgoing = jnp.take(parts, (me + shift) % size, axis=1)
        total = total + lax.ppermute(
            outgoing, "dp", [(i, (i + shift) % size) for i in range(size)]
        ).astype(jnp.float32)
    return total.astype(jnp.bfloat16)


def local(tokens, cotangent, gates, experts_hit, positions, gate_w, up_w, down_w):
    width = lax.axis_size("expert")
    rows_dev, routes = experts_hit.shape
    slots = width * CAP
    narrow = tokens.shape[1]
    valid = experts_hit >= 0
    flat = jnp.where(valid, experts_hit * CAP + positions, slots)
    slot_ids = jnp.arange(slots, dtype=jnp.int32)
    hit = flat[None, :, :] == slot_ids[:, None, None]
    onehot = jnp.any(hit, axis=2).astype(jnp.bfloat16)
    slot_gate = jnp.sum(
        jnp.where(hit, gates.astype(jnp.float32)[None, :, :], 0.0), axis=(1, 2)
    ).astype(jnp.bfloat16)
    packed_x = jnp.dot(onehot, tokens, preferred_element_type=jnp.float32).astype(jnp.bfloat16)
    packed_dy = jnp.dot(onehot, cotangent, preferred_element_type=jnp.float32).astype(jnp.bfloat16)
    gate_row = jnp.pad(slot_gate.reshape(width, 1, CAP), ((0, 0), (0, 0), (0, narrow - CAP)))
    block = jnp.concatenate(
        [
            packed_x.reshape(width, CAP, narrow),
            gate_row,
            packed_dy.reshape(width, CAP, narrow),
            jnp.zeros_like(gate_row),
        ],
        axis=1,
    )
    recv = lax.all_to_all(block, "expert", split_axis=0, concat_axis=0, tiled=True)
    recv_gate = recv[:, CAP, :CAP].reshape(slots)
    pair = jnp.stack(
        [
            recv[:, :CAP, :].reshape(slots, narrow),
            recv[:, CAP + 1 : 2 * CAP + 1, :].reshape(slots, narrow),
        ],
        axis=0,
    )
    full = lax.all_gather(pair, "etp", axis=2, tiled=True)
    stack = jnp.stack([gate_w[0], up_w[0], down_w[0].T], axis=0)
    d_part_b, term_b = expert_kernel(lax.axis_index("dp"), full, recv_gate, pieces_dp(stack))
    down_grad = scatter_sum_dp(term_b)[None]
    summed = lax.psum_scatter(d_part_b, "etp", scatter_dimension=1, tiled=True)
    returned = lax.all_to_all(
        summed.reshape(width, CAP, narrow), "expert", split_axis=0, concat_axis=0, tiled=True
    ).reshape(slots, narrow)
    total = lax.dot_general(
        onehot, returned, (((0,), (0,)), ((), ())), preferred_element_type=jnp.float32
    )
    input_grad = total.astype(jnp.bfloat16)
    return (input_grad, down_grad)


def solution(mesh):
    placed = (
        P(("dp", "expert"), "etp"),
        P(("dp", "expert"), "etp"),
        P(("dp", "expert"), None),
        P(("dp", "expert"), None),
        P(("dp", "expert"), None),
        P("expert", "dp", "etp"),
        P("expert", "dp", "etp"),
        P("expert", "etp", "dp"),
    )
    return jax.shard_map(
        local,
        mesh=mesh,
        in_specs=placed,
        out_specs=(P(("dp", "expert"), "etp"), P("expert", "etp", "dp")),
        check_vma=False,
    )
```

```python
import jax
import jax.numpy as jnp
from jax import lax
from jax.experimental import pallas as pl
from jax.experimental.pallas import tpu as pltpu
from jax.sharding import PartitionSpec as P

CAP = 19


def _expert_kernel(me_ref, rows_ref, gate_ref, *refs):
    size = len(refs) - 2
    w_refs = refs[:size]
    q_ref, term_ref = refs[size:]
    quarter = w_refs[0].shape[2]
    me = me_ref[0]
    nt = (((1,), (1,)), ((), ()))
    gate_pre = None
    for k in range(size):
        start = pl.multiple_of(((me + size - k) % size) * quarter, quarter)
        f_k = rows_ref[0, :, pl.ds(start, quarter)]
        g_k = rows_ref[1, :, pl.ds(start, quarter)]
        a = lax.dot_general(f_k, w_refs[k][0], nt, preferred_element_type=jnp.float32)
        b = lax.dot_general(f_k, w_refs[k][1], nt, preferred_element_type=jnp.float32)
        c = lax.dot_general(g_k, w_refs[k][2], nt, preferred_element_type=jnp.float32)
        if gate_pre is None:
            gate_pre, up_pre, back = a, b, c
        else:
            gate_pre, up_pre, back = gate_pre + a, up_pre + b, back + c
    sig = jax.nn.sigmoid(gate_pre)
    act = gate_pre * sig
    hidden = act * up_pre
    gate_f = gate_ref[...].astype(jnp.float32)
    d_hidden = gate_f * back
    d_gate_b = (d_hidden * up_pre * sig * (1.0 + gate_pre * (1.0 - sig))).astype(jnp.bfloat16)
    d_up_b = (d_hidden * act).astype(jnp.bfloat16)
    for k in range(size):
        start = pl.multiple_of(((me + size - k) % size) * quarter, quarter)
        part = jnp.dot(d_gate_b, w_refs[k][0], preferred_element_type=jnp.float32)
        part = part + jnp.dot(d_up_b, w_refs[k][1], preferred_element_type=jnp.float32)
        q_ref[:, pl.ds(start, quarter)] = part.astype(jnp.bfloat16)
    hidden_t = hidden.T.astype(jnp.bfloat16)
    scaled = (gate_f * rows_ref[1].astype(jnp.float32)).astype(jnp.bfloat16)
    term_ref[...] = jnp.dot(hidden_t, scaled, preferred_element_type=jnp.float32).astype(
        jnp.bfloat16
    )


def expert_kernel(me, rows, gate_col, pieces):
    _, slots, width = rows.shape
    ffb = pieces[0].shape[1]
    vmem = pltpu.VMEM
    return pl.pallas_call(
        _expert_kernel,
        out_shape=(
            jax.ShapeDtypeStruct((slots, width), jnp.bfloat16),
            jax.ShapeDtypeStruct((ffb, width), jnp.bfloat16),
        ),
        in_specs=[pl.BlockSpec(memory_space=pltpu.SMEM)]
        + [pl.BlockSpec(memory_space=vmem)] * (2 + len(pieces)),
        out_specs=(pl.BlockSpec(memory_space=vmem), pl.BlockSpec(memory_space=vmem)),
        compiler_params=pltpu.CompilerParams(vmem_limit_bytes=48 * 1024 * 1024),
    )(me.reshape(1), rows, gate_col.reshape(slots, 1), *pieces)


def pieces_dp(piece):
    size = lax.axis_size("dp")
    got = [piece]
    for shift in range(1, size):
        got.append(lax.ppermute(piece, "dp", [(i, (i + shift) % size) for i in range(size)]))
    return got


def scatter_sum_dp(term_b):
    size = lax.axis_size("dp")
    me = lax.axis_index("dp")
    quarter = term_b.shape[1] // size
    parts = term_b.reshape(term_b.shape[0], size, quarter)
    total = jnp.take(parts, me, axis=1).astype(jnp.float32)
    for shift in range(1, size):
        outgoing = jnp.take(parts, (me + shift) % size, axis=1)
        total = total + lax.ppermute(
            outgoing, "dp", [(i, (i + shift) % size) for i in range(size)]
        ).astype(jnp.float32)
    return total.astype(jnp.bfloat16)


def local(tokens, cotangent, gates, experts_hit, positions, gate_w, up_w, down_w):
    width = lax.axis_size("expert")
    rows_dev, routes = experts_hit.shape
    slots = width * CAP
    narrow = tokens.shape[1]
    valid = experts_hit >= 0
    flat = jnp.where(valid, experts_hit * CAP + positions, slots)
    slot_ids = jnp.arange(slots, dtype=jnp.int32)
    hit = flat[None, :, :] == slot_ids[:, None, None]
    onehot = jnp.any(hit, axis=2).astype(jnp.bfloat16)
    slot_gate = jnp.sum(
        jnp.where(hit, gates.astype(jnp.float32)[None, :, :], 0.0), axis=(1, 2)
    ).astype(jnp.bfloat16)
    packed_x = jnp.dot(onehot, tokens, preferred_element_type=jnp.float32).astype(jnp.bfloat16)
    packed_dy = jnp.dot(onehot, cotangent, preferred_element_type=jnp.float32).astype(jnp.bfloat16)
    gate_row = jnp.pad(slot_gate.reshape(width, 1, CAP), ((0, 0), (0, 0), (0, narrow - CAP)))
    block = jnp.concatenate(
        [
            packed_x.reshape(width, CAP, narrow),
            gate_row,
            packed_dy.reshape(width, CAP, narrow),
            jnp.zeros_like(gate_row),
        ],
        axis=1,
    )
    recv = lax.all_to_all(block, "expert", split_axis=0, concat_axis=0, tiled=True)
    recv_gate = recv[:, CAP, :CAP].reshape(slots)
    pair = jnp.stack(
        [
            recv[:, :CAP, :].reshape(slots, narrow),
            recv[:, CAP + 1 : 2 * CAP + 1, :].reshape(slots, narrow),
        ],
        axis=0,
    )
    full = lax.all_gather(pair, "etp", axis=2, tiled=True)
    stack = jnp.stack([gate_w[0].T, up_w[0].T, down_w[0]], axis=0)
    d_part_b, term_b = expert_kernel(lax.axis_index("dp"), full, recv_gate, pieces_dp(stack))
    down_grad = scatter_sum_dp(term_b)[None]
    summed = lax.psum_scatter(d_part_b, "etp", scatter_dimension=1, tiled=True)
    returned = lax.all_to_all(
        summed.reshape(width, CAP, narrow), "expert", split_axis=0, concat_axis=0, tiled=True
    ).reshape(slots, narrow)
    total = lax.dot_general(
        onehot, returned, (((0,), (0,)), ((), ())), preferred_element_type=jnp.float32
    )
    input_grad = total.astype(jnp.bfloat16)
    return (input_grad, down_grad)


def solution(mesh):
    placed = (
        P(("dp", "expert"), "etp"),
        P(("dp", "expert"), "etp"),
        P(("dp", "expert"), None),
        P(("dp", "expert"), None),
        P(("dp", "expert"), None),
        P("expert", "dp", "etp"),
        P("expert", "dp", "etp"),
        P("expert", "etp", "dp"),
    )
    return jax.shard_map(
        local,
        mesh=mesh,
        in_specs=placed,
        out_specs=(P(("dp", "expert"), "etp"), P("expert", "etp", "dp")),
        check_vma=False,
    )
```

```python
import functools

import jax
import jax.numpy as jnp
from jax import lax
from jax.experimental import pallas as pl
from jax.experimental.pallas import tpu as pltpu
from jax.sharding import PartitionSpec as P

CAP = 19


def _expert_kernel(me_ref, rows_ref, gate_ref, *refs, size, carry):
    w_refs = refs[:size]
    acc_ref = refs[size] if carry else None
    q_ref, term_ref = refs[-2:]
    quarter = w_refs[0].shape[2]
    me = me_ref[0]
    nt = (((1,), (1,)), ((), ()))
    gate_pre = None
    for k in range(size):
        start = pl.multiple_of(((me + size - k) % size) * quarter, quarter)
        f_k = rows_ref[0, :, pl.ds(start, quarter)]
        g_k = rows_ref[1, :, pl.ds(start, quarter)]
        a = lax.dot_general(f_k, w_refs[k][0], nt, preferred_element_type=jnp.float32)
        b = lax.dot_general(f_k, w_refs[k][1], nt, preferred_element_type=jnp.float32)
        c = lax.dot_general(g_k, w_refs[k][2], nt, preferred_element_type=jnp.float32)
        if gate_pre is None:
            gate_pre, up_pre, back = a, b, c
        else:
            gate_pre, up_pre, back = gate_pre + a, up_pre + b, back + c
    sig = jax.nn.sigmoid(gate_pre)
    act = gate_pre * sig
    hidden = act * up_pre
    gate_f = gate_ref[...].astype(jnp.float32)
    d_hidden = gate_f * back
    d_gate_b = (d_hidden * up_pre * sig * (1.0 + gate_pre * (1.0 - sig))).astype(jnp.bfloat16)
    d_up_b = (d_hidden * act).astype(jnp.bfloat16)
    for k in range(size):
        start = pl.multiple_of(((me + size - k) % size) * quarter, quarter)
        part = jnp.dot(d_gate_b, w_refs[k][0], preferred_element_type=jnp.float32)
        part = part + jnp.dot(d_up_b, w_refs[k][1], preferred_element_type=jnp.float32)
        q_ref[:, pl.ds(start, quarter)] = part.astype(jnp.bfloat16)
    hidden_t = hidden.T.astype(jnp.bfloat16)
    scaled = (gate_f * rows_ref[1].astype(jnp.float32)).astype(jnp.bfloat16)
    term = jnp.dot(hidden_t, scaled, preferred_element_type=jnp.float32)
    if carry:
        term = term + acc_ref[...]
    term_ref[...] = term.astype(term_ref.dtype)


def expert_kernel(me, rows, gate_col, pieces, acc=None):
    _, slots, width = rows.shape
    ffb = pieces[0].shape[1]
    vmem = pltpu.VMEM
    extra = [] if acc is None else [acc]
    return pl.pallas_call(
        functools.partial(_expert_kernel, size=len(pieces), carry=acc is not None),
        out_shape=(
            jax.ShapeDtypeStruct((slots, width), jnp.bfloat16),
            jax.ShapeDtypeStruct((ffb, width), jnp.float32 if acc is None else jnp.bfloat16),
        ),
        in_specs=[pl.BlockSpec(memory_space=pltpu.SMEM)]
        + [pl.BlockSpec(memory_space=vmem)] * (2 + len(pieces) + len(extra)),
        out_specs=(pl.BlockSpec(memory_space=vmem), pl.BlockSpec(memory_space=vmem)),
        compiler_params=pltpu.CompilerParams(vmem_limit_bytes=48 * 1024 * 1024),
    )(me.reshape(1), rows, gate_col.reshape(slots, 1), *pieces, *extra)


def pieces_dp(piece):
    size = lax.axis_size("dp")
    got = [piece]
    for shift in range(1, size):
        got.append(lax.ppermute(piece, "dp", [(i, (i + shift) % size) for i in range(size)]))
    return got


def scatter_sum_dp(term_b):
    size = lax.axis_size("dp")
    me = lax.axis_index("dp")
    quarter = term_b.shape[1] // size
    parts = term_b.reshape(term_b.shape[0], size, quarter)
    total = jnp.take(parts, me, axis=1).astype(jnp.float32)
    for shift in range(1, size):
        outgoing = jnp.take(parts, (me + shift) % size, axis=1)
        total = total + lax.ppermute(
            outgoing, "dp", [(i, (i + shift) % size) for i in range(size)]
        ).astype(jnp.float32)
    return total.astype(jnp.bfloat16)


def local(tokens, cotangent, gates, experts_hit, positions, gate_w, up_w, down_w):
    width = lax.axis_size("expert")
    rows_dev, routes = experts_hit.shape
    slots = width * CAP
    narrow = tokens.shape[1]
    valid = experts_hit >= 0
    flat = jnp.where(valid, experts_hit * CAP + positions, slots)
    slot_ids = jnp.arange(slots, dtype=jnp.int32)
    hit = flat[None, :, :] == slot_ids[:, None, None]
    onehot = jnp.any(hit, axis=2).astype(jnp.bfloat16)
    slot_gate = jnp.sum(
        jnp.where(hit, gates.astype(jnp.float32)[None, :, :], 0.0), axis=(1, 2)
    ).astype(jnp.bfloat16)
    packed_x = jnp.dot(onehot, tokens, preferred_element_type=jnp.float32).astype(jnp.bfloat16)
    packed_dy = jnp.dot(onehot, cotangent, preferred_element_type=jnp.float32).astype(jnp.bfloat16)
    packed_x = packed_x.reshape(width, CAP, narrow)
    packed_dy = packed_dy.reshape(width, CAP, narrow)
    gate_row = jnp.pad(slot_gate.reshape(width, 1, CAP), ((0, 0), (0, 0), (0, narrow - CAP)))
    cut = (CAP + 1) // 2
    spans = ((0, cut), (cut, CAP))
    stack = jnp.stack([gate_w[0].T, up_w[0].T, down_w[0]], axis=0)
    pieces = pieces_dp(stack)
    me = lax.axis_index("dp")
    acc = None
    returned = []
    recv_gate = None
    for idx, (lo, hi) in enumerate(spans):
        n = hi - lo
        parts = [packed_x[:, lo:hi], packed_dy[:, lo:hi]]
        if idx == 0:
            parts.append(gate_row)
        block = jnp.concatenate(parts, axis=1)
        recv = lax.all_to_all(block, "expert", split_axis=0, concat_axis=0, tiled=True)
        if idx == 0:
            recv_gate = recv[:, 2 * n, :CAP]
        pair = jnp.stack(
            [
                recv[:, :n, :].reshape(width * n, narrow),
                recv[:, n : 2 * n, :].reshape(width * n, narrow),
            ],
            axis=0,
        )
        full = lax.all_gather(pair, "etp", axis=2, tiled=True)
        gate_col = recv_gate[:, lo:hi].reshape(width * n)
        d_part_b, acc = expert_kernel(me, full, gate_col, pieces, acc)
        summed = lax.psum_scatter(d_part_b, "etp", scatter_dimension=1, tiled=True)
        returned.append(
            lax.all_to_all(
                summed.reshape(width, n, narrow), "expert", split_axis=0, concat_axis=0, tiled=True
            )
        )
    down_grad = scatter_sum_dp(acc)[None]
    table = jnp.concatenate(returned, axis=1).reshape(slots, narrow)
    total = lax.dot_general(
        onehot, table, (((0,), (0,)), ((), ())), preferred_element_type=jnp.float32
    )
    input_grad = total.astype(jnp.bfloat16)
    return (input_grad, down_grad)


def solution(mesh):
    placed = (
        P(("dp", "expert"), "etp"),
        P(("dp", "expert"), "etp"),
        P(("dp", "expert"), None),
        P(("dp", "expert"), None),
        P(("dp", "expert"), None),
        P("expert", "dp", "etp"),
        P("expert", "dp", "etp"),
        P("expert", "etp", "dp"),
    )
    return jax.shard_map(
        local,
        mesh=mesh,
        in_specs=placed,
        out_specs=(P(("dp", "expert"), "etp"), P("expert", "etp", "dp")),
        check_vma=False,
    )
```

```python
import jax
import jax.numpy as jnp
from jax import lax
from jax.experimental import pallas as pl
from jax.experimental.pallas import tpu as pltpu
from jax.sharding import PartitionSpec as P

CAP = 19


def _expert_kernel(me_ref, rows_ref, gate_ref, *refs):
    size = len(refs) - 2
    w_refs = refs[:size]
    q_ref, term_ref = refs[size:]
    quarter = w_refs[0].shape[2]
    narrow = q_ref.shape[2]
    me = me_ref[0]
    nt = (((1,), (1,)), ((), ()))
    gate_pre = None
    for k in range(size):
        start = pl.multiple_of(((me + size - k) % size) * quarter, quarter)
        f_k = rows_ref[0, :, pl.ds(start, quarter)]
        g_k = rows_ref[1, :, pl.ds(start, quarter)]
        a = lax.dot_general(f_k, w_refs[k][0], nt, preferred_element_type=jnp.float32)
        b = lax.dot_general(f_k, w_refs[k][1], nt, preferred_element_type=jnp.float32)
        c = lax.dot_general(g_k, w_refs[k][2], nt, preferred_element_type=jnp.float32)
        if gate_pre is None:
            gate_pre, up_pre, back = a, b, c
        else:
            gate_pre, up_pre, back = gate_pre + a, up_pre + b, back + c
    sig = jax.nn.sigmoid(gate_pre)
    act = gate_pre * sig
    hidden = act * up_pre
    gate_f = gate_ref[...].astype(jnp.float32)
    d_hidden = gate_f * back
    d_gate_b = (d_hidden * up_pre * sig * (1.0 + gate_pre * (1.0 - sig))).astype(jnp.bfloat16)
    d_up_b = (d_hidden * act).astype(jnp.bfloat16)
    for k in range(size):
        start = pl.multiple_of(((me + size - k) % size) * quarter, quarter)
        part = jnp.dot(d_gate_b, w_refs[k][0], preferred_element_type=jnp.float32)
        part = part + jnp.dot(d_up_b, w_refs[k][1], preferred_element_type=jnp.float32)
        part = part.astype(jnp.bfloat16)
        per = quarter // narrow
        block = ((me + size - k) % size) * per
        for h in range(per):
            q_ref[block + h] = part[:, h * narrow : (h + 1) * narrow]
    hidden_t = hidden.T.astype(jnp.bfloat16)
    scaled = (gate_f * rows_ref[1].astype(jnp.float32)).astype(jnp.bfloat16)
    term_ref[...] = jnp.dot(hidden_t, scaled, preferred_element_type=jnp.float32).astype(
        jnp.bfloat16
    )


def expert_kernel(me, rows, gate_col, pieces, split):
    _, slots, width = rows.shape
    ffb = pieces[0].shape[1]
    vmem = pltpu.VMEM
    return pl.pallas_call(
        _expert_kernel,
        out_shape=(
            jax.ShapeDtypeStruct((split, slots, width // split), jnp.bfloat16),
            jax.ShapeDtypeStruct((ffb, width), jnp.bfloat16),
        ),
        in_specs=[pl.BlockSpec(memory_space=pltpu.SMEM)]
        + [pl.BlockSpec(memory_space=vmem)] * (2 + len(pieces)),
        out_specs=(pl.BlockSpec(memory_space=vmem), pl.BlockSpec(memory_space=vmem)),
        compiler_params=pltpu.CompilerParams(vmem_limit_bytes=48 * 1024 * 1024),
    )(me.reshape(1), rows, gate_col.reshape(slots, 1), *pieces)


def pieces_dp(piece):
    size = lax.axis_size("dp")
    got = [piece]
    for shift in range(1, size):
        got.append(lax.ppermute(piece, "dp", [(i, (i + shift) % size) for i in range(size)]))
    return got


def scatter_sum_dp(term_b):
    size = lax.axis_size("dp")
    me = lax.axis_index("dp")
    quarter = term_b.shape[1] // size
    parts = term_b.reshape(term_b.shape[0], size, quarter)
    total = jnp.take(parts, me, axis=1).astype(jnp.float32)
    for shift in range(1, size):
        outgoing = jnp.take(parts, (me + shift) % size, axis=1)
        total = total + lax.ppermute(
            outgoing, "dp", [(i, (i + shift) % size) for i in range(size)]
        ).astype(jnp.float32)
    return total.astype(jnp.bfloat16)


def local(tokens, cotangent, gates, experts_hit, positions, gate_w, up_w, down_w):
    width = lax.axis_size("expert")
    rows_dev, routes = experts_hit.shape
    slots = width * CAP
    narrow = tokens.shape[1]
    valid = experts_hit >= 0
    flat = jnp.where(valid, experts_hit * CAP + positions, slots)
    slot_ids = jnp.arange(slots, dtype=jnp.int32)
    hit = flat[None, :, :] == slot_ids[:, None, None]
    onehot = jnp.any(hit, axis=2).astype(jnp.bfloat16)
    slot_gate = jnp.sum(
        jnp.where(hit, gates.astype(jnp.float32)[None, :, :], 0.0), axis=(1, 2)
    ).astype(jnp.bfloat16)
    packed_x = jnp.dot(onehot, tokens, preferred_element_type=jnp.float32).astype(jnp.bfloat16)
    packed_dy = jnp.dot(onehot, cotangent, preferred_element_type=jnp.float32).astype(jnp.bfloat16)
    gate_row = jnp.pad(slot_gate.reshape(width, 1, CAP), ((0, 0), (0, 0), (0, narrow - CAP)))
    block = jnp.concatenate(
        [
            packed_x.reshape(width, CAP, narrow),
            gate_row,
            packed_dy.reshape(width, CAP, narrow),
            jnp.zeros_like(gate_row),
        ],
        axis=1,
    )
    recv = lax.all_to_all(block, "expert", split_axis=0, concat_axis=0, tiled=True)
    recv_gate = recv[:, CAP, :CAP].reshape(slots)
    pair = jnp.stack(
        [
            recv[:, :CAP, :].reshape(slots, narrow),
            recv[:, CAP + 1 : 2 * CAP + 1, :].reshape(slots, narrow),
        ],
        axis=0,
    )
    full = lax.all_gather(pair, "etp", axis=2, tiled=True)
    stack = jnp.stack([gate_w[0].T, up_w[0].T, down_w[0]], axis=0)
    d_part_b, term_b = expert_kernel(
        lax.axis_index("dp"), full, recv_gate, pieces_dp(stack), lax.axis_size("etp")
    )
    down_grad = scatter_sum_dp(term_b)[None]
    summed = lax.psum_scatter(d_part_b, "etp", scatter_dimension=0, tiled=True)[0]
    returned = lax.all_to_all(
        summed.reshape(width, CAP, narrow), "expert", split_axis=0, concat_axis=0, tiled=True
    ).reshape(slots, narrow)
    total = lax.dot_general(
        onehot, returned, (((0,), (0,)), ((), ())), preferred_element_type=jnp.float32
    )
    input_grad = total.astype(jnp.bfloat16)
    return (input_grad, down_grad)


def solution(mesh):
    placed = (
        P(("dp", "expert"), "etp"),
        P(("dp", "expert"), "etp"),
        P(("dp", "expert"), None),
        P(("dp", "expert"), None),
        P(("dp", "expert"), None),
        P("expert", "dp", "etp"),
        P("expert", "dp", "etp"),
        P("expert", "etp", "dp"),
    )
    return jax.shard_map(
        local,
        mesh=mesh,
        in_specs=placed,
        out_specs=(P(("dp", "expert"), "etp"), P("expert", "etp", "dp")),
        check_vma=False,
    )
```

```python
import jax
import jax.numpy as jnp
from jax import lax
from jax.experimental import pallas as pl
from jax.experimental.pallas import tpu as pltpu
from jax.sharding import PartitionSpec as P

CAP = 19


def _expert_kernel(me_ref, rows_ref, gate_ref, *refs):
    size = len(refs) - 2
    w_refs = refs[:size]
    q_ref, hidden_ref = refs[size:]
    quarter = w_refs[0].shape[2]
    me = me_ref[0]
    nt = (((1,), (1,)), ((), ()))
    gate_pre = None
    for k in range(size):
        start = pl.multiple_of(((me + size - k) % size) * quarter, quarter)
        f_k = rows_ref[0, :, pl.ds(start, quarter)]
        g_k = rows_ref[1, :, pl.ds(start, quarter)]
        a = lax.dot_general(f_k, w_refs[k][0], nt, preferred_element_type=jnp.float32)
        b = lax.dot_general(f_k, w_refs[k][1], nt, preferred_element_type=jnp.float32)
        c = lax.dot_general(g_k, w_refs[k][2], nt, preferred_element_type=jnp.float32)
        if gate_pre is None:
            gate_pre, up_pre, back = a, b, c
        else:
            gate_pre, up_pre, back = gate_pre + a, up_pre + b, back + c
    sig = jax.nn.sigmoid(gate_pre)
    act = gate_pre * sig
    hidden = act * up_pre
    gate_f = gate_ref[...].astype(jnp.float32)
    d_hidden = gate_f * back
    d_gate_b = (d_hidden * up_pre * sig * (1.0 + gate_pre * (1.0 - sig))).astype(jnp.bfloat16)
    d_up_b = (d_hidden * act).astype(jnp.bfloat16)
    for k in range(size):
        start = pl.multiple_of(((me + size - k) % size) * quarter, quarter)
        part = jnp.dot(d_gate_b, w_refs[k][0], preferred_element_type=jnp.float32)
        part = part + jnp.dot(d_up_b, w_refs[k][1], preferred_element_type=jnp.float32)
        q_ref[:, pl.ds(start, quarter)] = part.astype(jnp.bfloat16)
    hidden_ref[...] = hidden.astype(jnp.bfloat16)


def expert_kernel(me, rows, gate_col, pieces):
    _, slots, width = rows.shape
    ffb = pieces[0].shape[1]
    vmem = pltpu.VMEM
    return pl.pallas_call(
        _expert_kernel,
        out_shape=(
            jax.ShapeDtypeStruct((slots, width), jnp.bfloat16),
            jax.ShapeDtypeStruct((slots, ffb), jnp.bfloat16),
        ),
        in_specs=[pl.BlockSpec(memory_space=pltpu.SMEM)]
        + [pl.BlockSpec(memory_space=vmem)] * (2 + len(pieces)),
        out_specs=(pl.BlockSpec(memory_space=vmem), pl.BlockSpec(memory_space=vmem)),
        compiler_params=pltpu.CompilerParams(vmem_limit_bytes=48 * 1024 * 1024),
    )(me.reshape(1), rows, gate_col.reshape(slots, 1), *pieces)


def pieces_dp(piece):
    size = lax.axis_size("dp")
    got = [piece]
    for shift in range(1, size):
        got.append(lax.ppermute(piece, "dp", [(i, (i + shift) % size) for i in range(size)]))
    return got


def scatter_sum_dp(term_b):
    size = lax.axis_size("dp")
    me = lax.axis_index("dp")
    quarter = term_b.shape[1] // size
    parts = term_b.reshape(term_b.shape[0], size, quarter)
    total = jnp.take(parts, me, axis=1).astype(jnp.float32)
    for shift in range(1, size):
        outgoing = jnp.take(parts, (me + shift) % size, axis=1)
        total = total + lax.ppermute(
            outgoing, "dp", [(i, (i + shift) % size) for i in range(size)]
        ).astype(jnp.float32)
    return total.astype(jnp.bfloat16)


def local(tokens, cotangent, gates, experts_hit, positions, gate_w, up_w, down_w):
    width = lax.axis_size("expert")
    rows_dev, routes = experts_hit.shape
    slots = width * CAP
    narrow = tokens.shape[1]
    valid = experts_hit >= 0
    flat = jnp.where(valid, experts_hit * CAP + positions, slots)
    slot_ids = jnp.arange(slots, dtype=jnp.int32)
    hit = flat[None, :, :] == slot_ids[:, None, None]
    onehot = jnp.any(hit, axis=2).astype(jnp.bfloat16)
    slot_gate = jnp.sum(
        jnp.where(hit, gates.astype(jnp.float32)[None, :, :], 0.0), axis=(1, 2)
    ).astype(jnp.bfloat16)
    packed_x = jnp.dot(onehot, tokens, preferred_element_type=jnp.float32).astype(jnp.bfloat16)
    packed_dy = jnp.dot(onehot, cotangent, preferred_element_type=jnp.float32).astype(jnp.bfloat16)
    gate_row = jnp.pad(slot_gate.reshape(width, 1, CAP), ((0, 0), (0, 0), (0, narrow - CAP)))
    block = jnp.concatenate(
        [
            packed_x.reshape(width, CAP, narrow),
            gate_row,
            packed_dy.reshape(width, CAP, narrow),
            jnp.zeros_like(gate_row),
        ],
        axis=1,
    )
    recv = lax.all_to_all(block, "expert", split_axis=0, concat_axis=0, tiled=True)
    recv_gate = recv[:, CAP, :CAP].reshape(slots)
    pair = jnp.stack(
        [
            recv[:, :CAP, :].reshape(slots, narrow),
            recv[:, CAP + 1 : 2 * CAP + 1, :].reshape(slots, narrow),
        ],
        axis=0,
    )
    full = lax.all_gather(pair, "etp", axis=2, tiled=True)
    stack = jnp.stack([gate_w[0].T, up_w[0].T, down_w[0]], axis=0)
    d_part_b, hidden_b = expert_kernel(lax.axis_index("dp"), full, recv_gate, pieces_dp(stack))
    summed = lax.psum_scatter(d_part_b, "etp", scatter_dimension=1, tiled=True)
    scaled = (recv_gate.astype(jnp.float32)[:, None] * full[1].astype(jnp.float32)).astype(
        jnp.bfloat16
    )
    term = lax.dot_general(
        hidden_b, scaled, (((0,), (0,)), ((), ())), preferred_element_type=jnp.float32
    )
    down_grad = scatter_sum_dp(term.astype(jnp.bfloat16))[None]
    returned = lax.all_to_all(
        summed.reshape(width, CAP, narrow), "expert", split_axis=0, concat_axis=0, tiled=True
    ).reshape(slots, narrow)
    total = lax.dot_general(
        onehot, returned, (((0,), (0,)), ((), ())), preferred_element_type=jnp.float32
    )
    input_grad = total.astype(jnp.bfloat16)
    return (input_grad, down_grad)


def solution(mesh):
    placed = (
        P(("dp", "expert"), "etp"),
        P(("dp", "expert"), "etp"),
        P(("dp", "expert"), None),
        P(("dp", "expert"), None),
        P(("dp", "expert"), None),
        P("expert", "dp", "etp"),
        P("expert", "dp", "etp"),
        P("expert", "etp", "dp"),
    )
    return jax.shard_map(
        local,
        mesh=mesh,
        in_specs=placed,
        out_specs=(P(("dp", "expert"), "etp"), P("expert", "etp", "dp")),
        check_vma=False,
    )
```

```python
import jax
import jax.numpy as jnp
from jax import lax
from jax.experimental import pallas as pl
from jax.experimental.pallas import tpu as pltpu
from jax.sharding import PartitionSpec as P

CAP = 19


def _expert_kernel(me_ref, x_ref, dy_ref, gate_ref, *refs):
    size = len(refs) - 2
    w_refs = refs[:size]
    q_ref, hidden_ref = refs[size:]
    quarter = w_refs[0].shape[2]
    me = me_ref[0]
    nt = (((1,), (1,)), ((), ()))
    gate_pre = None
    for k in range(size):
        start = pl.multiple_of(((me + size - k) % size) * quarter, quarter)
        f_k = x_ref[:, pl.ds(start, quarter)]
        g_k = dy_ref[:, pl.ds(start, quarter)]
        a = lax.dot_general(f_k, w_refs[k][0], nt, preferred_element_type=jnp.float32)
        b = lax.dot_general(f_k, w_refs[k][1], nt, preferred_element_type=jnp.float32)
        c = lax.dot_general(g_k, w_refs[k][2], nt, preferred_element_type=jnp.float32)
        if gate_pre is None:
            gate_pre, up_pre, back = a, b, c
        else:
            gate_pre, up_pre, back = gate_pre + a, up_pre + b, back + c
    sig = jax.nn.sigmoid(gate_pre)
    act = gate_pre * sig
    hidden = act * up_pre
    gate_f = gate_ref[...].astype(jnp.float32)
    d_hidden = gate_f * back
    d_gate_b = (d_hidden * up_pre * sig * (1.0 + gate_pre * (1.0 - sig))).astype(jnp.bfloat16)
    d_up_b = (d_hidden * act).astype(jnp.bfloat16)
    for k in range(size):
        start = pl.multiple_of(((me + size - k) % size) * quarter, quarter)
        part = jnp.dot(d_gate_b, w_refs[k][0], preferred_element_type=jnp.float32)
        part = part + jnp.dot(d_up_b, w_refs[k][1], preferred_element_type=jnp.float32)
        q_ref[:, pl.ds(start, quarter)] = part.astype(jnp.bfloat16)
    hidden_ref[...] = hidden.astype(jnp.bfloat16)


def expert_kernel(me, feats, grads, gate_col, pieces):
    slots, width = feats.shape
    ffb = pieces[0].shape[1]
    vmem = pltpu.VMEM
    return pl.pallas_call(
        _expert_kernel,
        out_shape=(
            jax.ShapeDtypeStruct((slots, width), jnp.bfloat16),
            jax.ShapeDtypeStruct((slots, ffb), jnp.bfloat16),
        ),
        in_specs=[pl.BlockSpec(memory_space=pltpu.SMEM)]
        + [pl.BlockSpec(memory_space=vmem)] * (3 + len(pieces)),
        out_specs=(pl.BlockSpec(memory_space=vmem), pl.BlockSpec(memory_space=vmem)),
        compiler_params=pltpu.CompilerParams(vmem_limit_bytes=48 * 1024 * 1024),
    )(me.reshape(1), feats, grads, gate_col.reshape(slots, 1), *pieces)


def shift(value, axis, step):
    size = lax.axis_size(axis)
    return lax.ppermute(value, axis, [(i, (i + step) % size) for i in range(size)])


def pieces_dp(piece):
    assert lax.axis_size("dp") == 4
    half = piece.shape[-1] // 2
    from_left = shift(piece, "dp", 1)
    from_right = shift(piece, "dp", -1)
    far = jnp.concatenate(
        [shift(from_left[..., :half], "dp", 1), shift(from_right[..., half:], "dp", -1)], axis=-1
    )
    return [piece, from_left, far, from_right]


def ring_gather_etp(block):
    size = lax.axis_size("etp")
    me = lax.axis_index("etp")
    narrow = block.shape[-1]
    out = jnp.zeros(block.shape[:-1] + (size * narrow,), block.dtype)
    out = lax.dynamic_update_slice_in_dim(out, block, me * narrow, axis=1)
    right = block
    left = block
    for step in range(1, size // 2 + 1):
        right = shift(right, "etp", 1)
        out = lax.dynamic_update_slice_in_dim(out, right, ((me - step) % size) * narrow, axis=1)
        if step < size - size // 2:
            left = shift(left, "etp", -1)
            out = lax.dynamic_update_slice_in_dim(out, left, ((me + step) % size) * narrow, axis=1)
    return out


def scatter_sum_dp(term_b):
    size = lax.axis_size("dp")
    me = lax.axis_index("dp")
    quarter = term_b.shape[1] // size
    parts = term_b.reshape(term_b.shape[0], size, quarter)
    total = jnp.take(parts, me, axis=1).astype(jnp.float32)
    for shift in range(1, size):
        outgoing = jnp.take(parts, (me + shift) % size, axis=1)
        total = total + lax.ppermute(
            outgoing, "dp", [(i, (i + shift) % size) for i in range(size)]
        ).astype(jnp.float32)
    return total.astype(jnp.bfloat16)


def local(tokens, cotangent, gates, experts_hit, positions, gate_w, up_w, down_w):
    width = lax.axis_size("expert")
    rows_dev, routes = experts_hit.shape
    slots = width * CAP
    narrow = tokens.shape[1]
    valid = experts_hit >= 0
    flat = jnp.where(valid, experts_hit * CAP + positions, slots)
    slot_ids = jnp.arange(slots, dtype=jnp.int32)
    hit = flat[None, :, :] == slot_ids[:, None, None]
    onehot = jnp.any(hit, axis=2).astype(jnp.bfloat16)
    slot_gate = jnp.sum(
        jnp.where(hit, gates.astype(jnp.float32)[None, :, :], 0.0), axis=(1, 2)
    ).astype(jnp.bfloat16)
    packed_x = jnp.dot(onehot, tokens, preferred_element_type=jnp.float32).astype(jnp.bfloat16)
    packed_dy = jnp.dot(onehot, cotangent, preferred_element_type=jnp.float32).astype(jnp.bfloat16)
    gate_row = jnp.pad(slot_gate.reshape(width, 1, CAP), ((0, 0), (0, 0), (0, narrow - CAP)))
    block = jnp.concatenate(
        [
            packed_x.reshape(width, CAP, narrow),
            gate_row,
            packed_dy.reshape(width, CAP, narrow),
            jnp.zeros_like(gate_row),
        ],
        axis=1,
    )
    recv = lax.all_to_all(block, "expert", split_axis=0, concat_axis=0, tiled=True)
    recv_gate = recv[:, CAP, :CAP].reshape(slots)
    feats = lax.all_gather(recv[:, :CAP, :].reshape(slots, narrow), "etp", axis=1, tiled=True)
    grads = ring_gather_etp(recv[:, CAP + 1 : 2 * CAP + 1, :].reshape(slots, narrow))
    stack = jnp.stack([gate_w[0].T, up_w[0].T, down_w[0]], axis=0)
    d_part_b, hidden_b = expert_kernel(
        lax.axis_index("dp"), feats, grads, recv_gate, pieces_dp(stack)
    )
    summed = lax.psum_scatter(d_part_b, "etp", scatter_dimension=1, tiled=True)
    scaled = (recv_gate.astype(jnp.float32)[:, None] * grads.astype(jnp.float32)).astype(
        jnp.bfloat16
    )
    term = lax.dot_general(
        hidden_b, scaled, (((0,), (0,)), ((), ())), preferred_element_type=jnp.float32
    )
    down_grad = scatter_sum_dp(term.astype(jnp.bfloat16))[None]
    returned = lax.all_to_all(
        summed.reshape(width, CAP, narrow), "expert", split_axis=0, concat_axis=0, tiled=True
    ).reshape(slots, narrow)
    total = lax.dot_general(
        onehot, returned, (((0,), (0,)), ((), ())), preferred_element_type=jnp.float32
    )
    input_grad = total.astype(jnp.bfloat16)
    return (input_grad, down_grad)


def solution(mesh):
    placed = (
        P(("dp", "expert"), "etp"),
        P(("dp", "expert"), "etp"),
        P(("dp", "expert"), None),
        P(("dp", "expert"), None),
        P(("dp", "expert"), None),
        P("expert", "dp", "etp"),
        P("expert", "dp", "etp"),
        P("expert", "etp", "dp"),
    )
    return jax.shard_map(
        local,
        mesh=mesh,
        in_specs=placed,
        out_specs=(P(("dp", "expert"), "etp"), P("expert", "etp", "dp")),
        check_vma=False,
    )
```

```python
import jax
import jax.numpy as jnp
from jax import lax
from jax.experimental import pallas as pl
from jax.experimental.pallas import tpu as pltpu
from jax.sharding import PartitionSpec as P

CAP = 19


def _expert_kernel(me_ref, rows_ref, gate_ref, *refs):
    size = len(refs) - 2
    w_refs = refs[:size]
    q_ref, hidden_ref = refs[size:]
    quarter = w_refs[0].shape[2]
    me = me_ref[0]
    nt = (((1,), (1,)), ((), ()))
    gate_pre = None
    for k in range(size):
        start = pl.multiple_of(((me + size - k) % size) * quarter, quarter)
        f_k = rows_ref[0, :, pl.ds(start, quarter)]
        g_k = rows_ref[1, :, pl.ds(start, quarter)]
        a = lax.dot_general(f_k, w_refs[k][0], nt, preferred_element_type=jnp.float32)
        b = lax.dot_general(f_k, w_refs[k][1], nt, preferred_element_type=jnp.float32)
        c = lax.dot_general(g_k, w_refs[k][2], nt, preferred_element_type=jnp.float32)
        if gate_pre is None:
            gate_pre, up_pre, back = a, b, c
        else:
            gate_pre, up_pre, back = gate_pre + a, up_pre + b, back + c
    sig = jax.nn.sigmoid(gate_pre)
    act = gate_pre * sig
    hidden = act * up_pre
    gate_f = gate_ref[...].astype(jnp.float32)
    d_hidden = gate_f * back
    d_gate_b = (d_hidden * up_pre * sig * (1.0 + gate_pre * (1.0 - sig))).astype(jnp.bfloat16)
    d_up_b = (d_hidden * act).astype(jnp.bfloat16)
    for k in range(size):
        start = pl.multiple_of(((me + size - k) % size) * quarter, quarter)
        part = jnp.dot(d_gate_b, w_refs[k][0], preferred_element_type=jnp.float32)
        part = part + jnp.dot(d_up_b, w_refs[k][1], preferred_element_type=jnp.float32)
        q_ref[:, pl.ds(start, quarter)] = part.astype(jnp.bfloat16)
    hidden_ref[...] = hidden.astype(jnp.bfloat16)


def expert_kernel(me, rows, gate_col, pieces):
    _, slots, width = rows.shape
    ffb = pieces[0].shape[1]
    vmem = pltpu.VMEM
    return pl.pallas_call(
        _expert_kernel,
        out_shape=(
            jax.ShapeDtypeStruct((slots, width), jnp.bfloat16),
            jax.ShapeDtypeStruct((slots, ffb), jnp.bfloat16),
        ),
        in_specs=[pl.BlockSpec(memory_space=pltpu.SMEM)]
        + [pl.BlockSpec(memory_space=vmem)] * (2 + len(pieces)),
        out_specs=(pl.BlockSpec(memory_space=vmem), pl.BlockSpec(memory_space=vmem)),
        compiler_params=pltpu.CompilerParams(vmem_limit_bytes=48 * 1024 * 1024),
    )(me.reshape(1), rows, gate_col.reshape(slots, 1), *pieces)


def pieces_dp(piece):
    size = lax.axis_size("dp")
    got = [piece]
    for shift in range(1, size):
        got.append(lax.ppermute(piece, "dp", [(i, (i + shift) % size) for i in range(size)]))
    return got


def scatter_sum_dp(term_b):
    size = lax.axis_size("dp")
    me = lax.axis_index("dp")
    quarter = term_b.shape[1] // size
    parts = term_b.reshape(term_b.shape[0], size, quarter)
    total = jnp.take(parts, me, axis=1).astype(jnp.float32)
    for shift in range(1, size):
        outgoing = jnp.take(parts, (me + shift) % size, axis=1)
        total = total + lax.ppermute(
            outgoing, "dp", [(i, (i + shift) % size) for i in range(size)]
        ).astype(jnp.float32)
    return total.astype(jnp.bfloat16)


def local(tokens, cotangent, gates, experts_hit, positions, gate_w, up_w, down_w):
    width = lax.axis_size("expert")
    rows_dev, routes = experts_hit.shape
    slots = width * CAP
    narrow = tokens.shape[1]
    valid = experts_hit >= 0
    flat = jnp.where(valid, experts_hit * CAP + positions, slots)
    slot_ids = jnp.arange(slots, dtype=jnp.int32)
    flat_t = flat.T
    gates_t = gates.astype(jnp.float32).T
    filled = jnp.zeros((slots, rows_dev), jnp.bool_)
    gate_sum = jnp.zeros((slots, rows_dev), jnp.float32)
    for route in range(routes):
        hit = flat_t[route][None, :] == slot_ids[:, None]
        filled = filled | hit
        gate_sum = gate_sum + jnp.where(hit, gates_t[route][None, :], 0.0)
    onehot = filled.astype(jnp.bfloat16)
    slot_gate = jnp.sum(gate_sum, axis=1).astype(jnp.bfloat16)
    packed_x = jnp.dot(onehot, tokens, preferred_element_type=jnp.float32).astype(jnp.bfloat16)
    packed_dy = jnp.dot(onehot, cotangent, preferred_element_type=jnp.float32).astype(jnp.bfloat16)
    gate_row = jnp.pad(slot_gate.reshape(width, 1, CAP), ((0, 0), (0, 0), (0, narrow - CAP)))
    block = jnp.concatenate(
        [
            packed_x.reshape(width, CAP, narrow),
            gate_row,
            packed_dy.reshape(width, CAP, narrow),
            jnp.zeros_like(gate_row),
        ],
        axis=1,
    )
    recv = lax.all_to_all(block, "expert", split_axis=0, concat_axis=0, tiled=True)
    recv_gate = recv[:, CAP, :CAP].reshape(slots)
    pair = jnp.stack(
        [
            recv[:, :CAP, :].reshape(slots, narrow),
            recv[:, CAP + 1 : 2 * CAP + 1, :].reshape(slots, narrow),
        ],
        axis=0,
    )
    full = lax.all_gather(pair, "etp", axis=2, tiled=True)
    stack = jnp.stack([gate_w[0].T, up_w[0].T, down_w[0]], axis=0)
    d_part_b, hidden_b = expert_kernel(lax.axis_index("dp"), full, recv_gate, pieces_dp(stack))
    summed = lax.psum_scatter(d_part_b, "etp", scatter_dimension=1, tiled=True)
    scaled = (recv_gate.astype(jnp.float32)[:, None] * full[1].astype(jnp.float32)).astype(
        jnp.bfloat16
    )
    term = lax.dot_general(
        hidden_b, scaled, (((0,), (0,)), ((), ())), preferred_element_type=jnp.float32
    )
    down_grad = scatter_sum_dp(term.astype(jnp.bfloat16))[None]
    returned = lax.all_to_all(
        summed.reshape(width, CAP, narrow), "expert", split_axis=0, concat_axis=0, tiled=True
    ).reshape(slots, narrow)
    total = lax.dot_general(
        onehot, returned, (((0,), (0,)), ((), ())), preferred_element_type=jnp.float32
    )
    input_grad = total.astype(jnp.bfloat16)
    return (input_grad, down_grad)


def solution(mesh):
    placed = (
        P(("dp", "expert"), "etp"),
        P(("dp", "expert"), "etp"),
        P(("dp", "expert"), None),
        P(("dp", "expert"), None),
        P(("dp", "expert"), None),
        P("expert", "dp", "etp"),
        P("expert", "dp", "etp"),
        P("expert", "etp", "dp"),
    )
    return jax.shard_map(
        local,
        mesh=mesh,
        in_specs=placed,
        out_specs=(P(("dp", "expert"), "etp"), P("expert", "etp", "dp")),
        check_vma=False,
    )
```

```python
import jax
import jax.numpy as jnp
from jax import lax
from jax.experimental import pallas as pl
from jax.experimental.pallas import tpu as pltpu
from jax.sharding import PartitionSpec as P

CAP = 19


def _expert_kernel(me_ref, rows_ref, gate_ref, *refs):
    size = len(refs) - 2
    w_refs = refs[:size]
    q_ref, hidden_ref = refs[size:]
    quarter = w_refs[0].shape[2]
    me = me_ref[0]
    nt = (((1,), (1,)), ((), ()))
    gate_pre = None
    for k in range(size):
        start = pl.multiple_of(((me + size - k) % size) * quarter, quarter)
        f_k = rows_ref[0, :, pl.ds(start, quarter)]
        g_k = rows_ref[1, :, pl.ds(start, quarter)]
        a = lax.dot_general(f_k, w_refs[k][0], nt, preferred_element_type=jnp.float32)
        b = lax.dot_general(f_k, w_refs[k][1], nt, preferred_element_type=jnp.float32)
        c = lax.dot_general(g_k, w_refs[k][2], nt, preferred_element_type=jnp.float32)
        if gate_pre is None:
            gate_pre, up_pre, back = a, b, c
        else:
            gate_pre, up_pre, back = gate_pre + a, up_pre + b, back + c
    sig = jax.nn.sigmoid(gate_pre)
    act = gate_pre * sig
    hidden = act * up_pre
    gate_f = gate_ref[...].astype(jnp.float32)
    d_hidden = gate_f * back
    d_gate_b = (d_hidden * up_pre * sig * (1.0 + gate_pre * (1.0 - sig))).astype(jnp.bfloat16)
    d_up_b = (d_hidden * act).astype(jnp.bfloat16)
    for k in range(size):
        start = pl.multiple_of(((me + size - k) % size) * quarter, quarter)
        part = jnp.dot(d_gate_b, w_refs[k][0], preferred_element_type=jnp.float32)
        part = part + jnp.dot(d_up_b, w_refs[k][1], preferred_element_type=jnp.float32)
        q_ref[:, pl.ds(start, quarter)] = part.astype(jnp.bfloat16)
    hidden_ref[...] = hidden.astype(jnp.bfloat16)


def expert_kernel(me, rows, gate_col, pieces):
    _, slots, width = rows.shape
    ffb = pieces[0].shape[1]
    vmem = pltpu.VMEM
    return pl.pallas_call(
        _expert_kernel,
        out_shape=(
            jax.ShapeDtypeStruct((slots, width), jnp.bfloat16),
            jax.ShapeDtypeStruct((slots, ffb), jnp.bfloat16),
        ),
        in_specs=[pl.BlockSpec(memory_space=pltpu.SMEM)]
        + [pl.BlockSpec(memory_space=vmem)] * (2 + len(pieces)),
        out_specs=(pl.BlockSpec(memory_space=vmem), pl.BlockSpec(memory_space=vmem)),
        compiler_params=pltpu.CompilerParams(vmem_limit_bytes=48 * 1024 * 1024),
    )(me.reshape(1), rows, gate_col.reshape(slots, 1), *pieces)


def shift(value, axis, step):
    size = lax.axis_size(axis)
    return lax.ppermute(value, axis, [(i, (i + step) % size) for i in range(size)])


def pieces_dp(piece):
    assert lax.axis_size("dp") == 4
    half = piece.shape[-1] // 2
    from_left = shift(piece, "dp", 1)
    from_right = shift(piece, "dp", -1)
    far = jnp.concatenate(
        [shift(from_left[..., :half], "dp", 1), shift(from_right[..., half:], "dp", -1)], axis=-1
    )
    return [piece, from_left, far, from_right]


def scatter_sum_dp(term_b):
    size = lax.axis_size("dp")
    me = lax.axis_index("dp")
    quarter = term_b.shape[1] // size
    parts = term_b.reshape(term_b.shape[0], size, quarter)
    total = jnp.take(parts, me, axis=1).astype(jnp.float32)
    for shift in range(1, size):
        outgoing = jnp.take(parts, (me + shift) % size, axis=1)
        total = total + lax.ppermute(
            outgoing, "dp", [(i, (i + shift) % size) for i in range(size)]
        ).astype(jnp.float32)
    return total.astype(jnp.bfloat16)


def local(tokens, cotangent, gates, experts_hit, positions, gate_w, up_w, down_w):
    width = lax.axis_size("expert")
    rows_dev, routes = experts_hit.shape
    slots = width * CAP
    narrow = tokens.shape[1]
    valid = experts_hit >= 0
    flat = jnp.where(valid, experts_hit * CAP + positions, slots)
    slot_ids = jnp.arange(slots, dtype=jnp.int32)
    hit = flat[None, :, :] == slot_ids[:, None, None]
    onehot = jnp.any(hit, axis=2).astype(jnp.bfloat16)
    slot_gate = jnp.sum(
        jnp.where(hit, gates.astype(jnp.float32)[None, :, :], 0.0), axis=(1, 2)
    ).astype(jnp.bfloat16)
    packed_x = jnp.dot(onehot, tokens, preferred_element_type=jnp.float32).astype(jnp.bfloat16)
    packed_dy = jnp.dot(onehot, cotangent, preferred_element_type=jnp.float32).astype(jnp.bfloat16)
    gate_row = jnp.pad(slot_gate.reshape(width, 1, CAP), ((0, 0), (0, 0), (0, narrow - CAP)))
    block = jnp.concatenate(
        [
            packed_x.reshape(width, CAP, narrow),
            gate_row,
            packed_dy.reshape(width, CAP, narrow),
            jnp.zeros_like(gate_row),
        ],
        axis=1,
    )
    recv = lax.all_to_all(block, "expert", split_axis=0, concat_axis=0, tiled=True)
    recv_gate = recv[:, CAP, :CAP].reshape(slots)
    pair = jnp.stack(
        [
            recv[:, :CAP, :].reshape(slots, narrow),
            recv[:, CAP + 1 : 2 * CAP + 1, :].reshape(slots, narrow),
        ],
        axis=0,
    )
    full = lax.all_gather(pair, "etp", axis=2, tiled=True)
    stack = jnp.stack([gate_w[0].T, up_w[0].T, down_w[0]], axis=0)
    d_part_b, hidden_b = expert_kernel(lax.axis_index("dp"), full, recv_gate, pieces_dp(stack))
    summed = lax.psum_scatter(d_part_b, "etp", scatter_dimension=1, tiled=True)
    scaled = (recv_gate.astype(jnp.float32)[:, None] * full[1].astype(jnp.float32)).astype(
        jnp.bfloat16
    )
    term = lax.dot_general(
        hidden_b, scaled, (((0,), (0,)), ((), ())), preferred_element_type=jnp.float32
    )
    down_grad = scatter_sum_dp(term.astype(jnp.bfloat16))[None]
    returned = lax.all_to_all(
        summed.reshape(width, CAP, narrow), "expert", split_axis=0, concat_axis=0, tiled=True
    ).reshape(slots, narrow)
    total = lax.dot_general(
        onehot, returned, (((0,), (0,)), ((), ())), preferred_element_type=jnp.float32
    )
    input_grad = total.astype(jnp.bfloat16)
    return (input_grad, down_grad)


def solution(mesh):
    placed = (
        P(("dp", "expert"), "etp"),
        P(("dp", "expert"), "etp"),
        P(("dp", "expert"), None),
        P(("dp", "expert"), None),
        P(("dp", "expert"), None),
        P("expert", "dp", "etp"),
        P("expert", "dp", "etp"),
        P("expert", "etp", "dp"),
    )
    return jax.shard_map(
        local,
        mesh=mesh,
        in_specs=placed,
        out_specs=(P(("dp", "expert"), "etp"), P("expert", "etp", "dp")),
        check_vma=False,
    )
```

```python
import jax
import jax.numpy as jnp
from jax import lax
from jax.experimental import pallas as pl
from jax.experimental.pallas import tpu as pltpu
from jax.sharding import PartitionSpec as P

CAP = 19


def _expert_kernel(me_ref, rows_hbm, gate_ref, *refs):
    size = len(refs) - 5
    w_refs = refs[:size]
    q_hbm, hidden_ref, rows_buf, q_buf, sems = refs[size:]
    quarter = w_refs[0].shape[2]
    me = me_ref[0]
    nt = (((1,), (1,)), ((), ()))
    starts = [pl.multiple_of(((me + size - k) % size) * quarter, quarter) for k in range(size)]
    loads = []
    for k in range(size):
        cols = pl.ds(starts[k], quarter)
        copy = pltpu.make_async_copy(rows_hbm.at[:, :, cols], rows_buf.at[k], sems.at[0, k])
        copy.start()
        loads.append(copy)
    gate_pre = None
    for k in range(size):
        loads[k].wait()
        f_k = rows_buf[k, 0]
        g_k = rows_buf[k, 1]
        a = lax.dot_general(f_k, w_refs[k][0], nt, preferred_element_type=jnp.float32)
        b = lax.dot_general(f_k, w_refs[k][1], nt, preferred_element_type=jnp.float32)
        c = lax.dot_general(g_k, w_refs[k][2], nt, preferred_element_type=jnp.float32)
        if gate_pre is None:
            gate_pre, up_pre, back = a, b, c
        else:
            gate_pre, up_pre, back = gate_pre + a, up_pre + b, back + c
    sig = jax.nn.sigmoid(gate_pre)
    act = gate_pre * sig
    hidden = act * up_pre
    gate_f = gate_ref[...].astype(jnp.float32)
    d_hidden = gate_f * back
    d_gate_b = (d_hidden * up_pre * sig * (1.0 + gate_pre * (1.0 - sig))).astype(jnp.bfloat16)
    d_up_b = (d_hidden * act).astype(jnp.bfloat16)
    stores = []
    for k in range(size):
        part = jnp.dot(d_gate_b, w_refs[k][0], preferred_element_type=jnp.float32)
        part = part + jnp.dot(d_up_b, w_refs[k][1], preferred_element_type=jnp.float32)
        q_buf[k] = part.astype(jnp.bfloat16)
        copy = pltpu.make_async_copy(
            q_buf.at[k], q_hbm.at[:, pl.ds(starts[k], quarter)], sems.at[1, k]
        )
        copy.start()
        stores.append(copy)
    hidden_ref[...] = hidden.astype(jnp.bfloat16)
    for copy in stores:
        copy.wait()


def expert_kernel(me, rows, gate_col, pieces):
    _, slots, width = rows.shape
    ffb = pieces[0].shape[1]
    size = len(pieces)
    quarter = width // size
    vmem = pltpu.VMEM
    return pl.pallas_call(
        _expert_kernel,
        out_shape=(
            jax.ShapeDtypeStruct((slots, width), jnp.bfloat16),
            jax.ShapeDtypeStruct((slots, ffb), jnp.bfloat16),
        ),
        in_specs=[pl.BlockSpec(memory_space=pltpu.SMEM), pl.BlockSpec(memory_space=pl.ANY)]
        + [pl.BlockSpec(memory_space=vmem)] * (1 + size),
        out_specs=(pl.BlockSpec(memory_space=pl.ANY), pl.BlockSpec(memory_space=vmem)),
        scratch_shapes=[
            pltpu.VMEM((size, 2, slots, quarter), jnp.bfloat16),
            pltpu.VMEM((size, slots, quarter), jnp.bfloat16),
            pltpu.SemaphoreType.DMA((2, size)),
        ],
        compiler_params=pltpu.CompilerParams(vmem_limit_bytes=48 * 1024 * 1024),
    )(me.reshape(1), rows, gate_col.reshape(slots, 1), *pieces)


def pieces_dp(piece):
    size = lax.axis_size("dp")
    got = [piece]
    for shift in range(1, size):
        got.append(lax.ppermute(piece, "dp", [(i, (i + shift) % size) for i in range(size)]))
    return got


def scatter_sum_dp(term_b):
    size = lax.axis_size("dp")
    me = lax.axis_index("dp")
    quarter = term_b.shape[1] // size
    parts = term_b.reshape(term_b.shape[0], size, quarter)
    total = jnp.take(parts, me, axis=1).astype(jnp.float32)
    for shift in range(1, size):
        outgoing = jnp.take(parts, (me + shift) % size, axis=1)
        total = total + lax.ppermute(
            outgoing, "dp", [(i, (i + shift) % size) for i in range(size)]
        ).astype(jnp.float32)
    return total.astype(jnp.bfloat16)


def local(tokens, cotangent, gates, experts_hit, positions, gate_w, up_w, down_w):
    width = lax.axis_size("expert")
    rows_dev, routes = experts_hit.shape
    slots = width * CAP
    narrow = tokens.shape[1]
    valid = experts_hit >= 0
    flat = jnp.where(valid, experts_hit * CAP + positions, slots)
    slot_ids = jnp.arange(slots, dtype=jnp.int32)
    hit = flat[None, :, :] == slot_ids[:, None, None]
    onehot = jnp.any(hit, axis=2).astype(jnp.bfloat16)
    slot_gate = jnp.sum(
        jnp.where(hit, gates.astype(jnp.float32)[None, :, :], 0.0), axis=(1, 2)
    ).astype(jnp.bfloat16)
    packed_x = jnp.dot(onehot, tokens, preferred_element_type=jnp.float32).astype(jnp.bfloat16)
    packed_dy = jnp.dot(onehot, cotangent, preferred_element_type=jnp.float32).astype(jnp.bfloat16)
    gate_row = jnp.pad(slot_gate.reshape(width, 1, CAP), ((0, 0), (0, 0), (0, narrow - CAP)))
    block = jnp.concatenate(
        [
            packed_x.reshape(width, CAP, narrow),
            gate_row,
            packed_dy.reshape(width, CAP, narrow),
            jnp.zeros_like(gate_row),
        ],
        axis=1,
    )
    recv = lax.all_to_all(block, "expert", split_axis=0, concat_axis=0, tiled=True)
    recv_gate = recv[:, CAP, :CAP].reshape(slots)
    pair = jnp.stack(
        [
            recv[:, :CAP, :].reshape(slots, narrow),
            recv[:, CAP + 1 : 2 * CAP + 1, :].reshape(slots, narrow),
        ],
        axis=0,
    )
    full = lax.all_gather(pair, "etp", axis=2, tiled=True)
    stack = jnp.stack([gate_w[0].T, up_w[0].T, down_w[0]], axis=0)
    d_part_b, hidden_b = expert_kernel(lax.axis_index("dp"), full, recv_gate, pieces_dp(stack))
    summed = lax.psum_scatter(d_part_b, "etp", scatter_dimension=1, tiled=True)
    scaled = (recv_gate.astype(jnp.float32)[:, None] * full[1].astype(jnp.float32)).astype(
        jnp.bfloat16
    )
    term = lax.dot_general(
        hidden_b, scaled, (((0,), (0,)), ((), ())), preferred_element_type=jnp.float32
    )
    down_grad = scatter_sum_dp(term.astype(jnp.bfloat16))[None]
    returned = lax.all_to_all(
        summed.reshape(width, CAP, narrow), "expert", split_axis=0, concat_axis=0, tiled=True
    ).reshape(slots, narrow)
    total = lax.dot_general(
        onehot, returned, (((0,), (0,)), ((), ())), preferred_element_type=jnp.float32
    )
    input_grad = total.astype(jnp.bfloat16)
    return (input_grad, down_grad)


def solution(mesh):
    placed = (
        P(("dp", "expert"), "etp"),
        P(("dp", "expert"), "etp"),
        P(("dp", "expert"), None),
        P(("dp", "expert"), None),
        P(("dp", "expert"), None),
        P("expert", "dp", "etp"),
        P("expert", "dp", "etp"),
        P("expert", "etp", "dp"),
    )
    return jax.shard_map(
        local,
        mesh=mesh,
        in_specs=placed,
        out_specs=(P(("dp", "expert"), "etp"), P("expert", "etp", "dp")),
        check_vma=False,
    )
```

```python
import jax
import jax.numpy as jnp
from jax import lax
from jax.experimental import pallas as pl
from jax.experimental.pallas import tpu as pltpu
from jax.sharding import PartitionSpec as P

CAP = 19


def _expert_kernel(me_ref, rows_ref, gate_ref, *refs):
    size = len(refs) - 2
    w_refs = refs[:size]
    q_ref, hidden_ref = refs[size:]
    quarter = w_refs[0].shape[2]
    me = me_ref[0]
    nt = (((1,), (1,)), ((), ()))
    gate_pre = None
    for k in range(size):
        start = pl.multiple_of(((me + size - k) % size) * quarter, quarter)
        f_k = rows_ref[0, :, pl.ds(start, quarter)]
        g_k = rows_ref[1, :, pl.ds(start, quarter)]
        a = lax.dot_general(f_k, w_refs[k][0], nt, preferred_element_type=jnp.float32)
        b = lax.dot_general(f_k, w_refs[k][1], nt, preferred_element_type=jnp.float32)
        c = lax.dot_general(g_k, w_refs[k][2], nt, preferred_element_type=jnp.float32)
        if gate_pre is None:
            gate_pre, up_pre, back = a, b, c
        else:
            gate_pre, up_pre, back = gate_pre + a, up_pre + b, back + c
    sig = jax.nn.sigmoid(gate_pre)
    act = gate_pre * sig
    hidden = act * up_pre
    gate_f = gate_ref[...].astype(jnp.float32)
    d_hidden = gate_f * back
    d_gate_b = (d_hidden * up_pre * sig * (1.0 + gate_pre * (1.0 - sig))).astype(jnp.bfloat16)
    d_up_b = (d_hidden * act).astype(jnp.bfloat16)
    for k in range(size):
        start = pl.multiple_of(((me + size - k) % size) * quarter, quarter)
        part = jnp.dot(d_gate_b, w_refs[k][0], preferred_element_type=jnp.float32)
        part = part + jnp.dot(d_up_b, w_refs[k][1], preferred_element_type=jnp.float32)
        q_ref[:, pl.ds(start, quarter)] = part.astype(jnp.bfloat16)
    hidden_ref[...] = hidden.astype(jnp.bfloat16)


def expert_kernel(me, rows, gate_col, pieces):
    _, slots, width = rows.shape
    ffb = pieces[0].shape[1]
    vmem = pltpu.VMEM
    return pl.pallas_call(
        _expert_kernel,
        out_shape=(
            jax.ShapeDtypeStruct((slots, width), jnp.bfloat16),
            jax.ShapeDtypeStruct((slots, ffb), jnp.bfloat16),
        ),
        in_specs=[pl.BlockSpec(memory_space=pltpu.SMEM)]
        + [pl.BlockSpec(memory_space=vmem)] * (2 + len(pieces)),
        out_specs=(pl.BlockSpec(memory_space=vmem), pl.BlockSpec(memory_space=vmem)),
        compiler_params=pltpu.CompilerParams(vmem_limit_bytes=48 * 1024 * 1024),
    )(me.reshape(1), rows, gate_col.reshape(slots, 1), *pieces)


def pieces_dp(piece):
    size = lax.axis_size("dp")
    got = [piece]
    for shift in range(1, size):
        got.append(lax.ppermute(piece, "dp", [(i, (i + shift) % size) for i in range(size)]))
    return got


def scatter_sum_dp(term_b):
    size = lax.axis_size("dp")
    me = lax.axis_index("dp")
    quarter = term_b.shape[1] // size
    parts = term_b.reshape(term_b.shape[0], size, quarter)
    total = jnp.take(parts, me, axis=1).astype(jnp.float32)
    for shift in range(1, size):
        outgoing = jnp.take(parts, (me + shift) % size, axis=1)
        total = total + lax.ppermute(
            outgoing, "dp", [(i, (i + shift) % size) for i in range(size)]
        ).astype(jnp.float32)
    return total.astype(jnp.bfloat16)


def local(tokens, cotangent, gates, experts_hit, positions, gate_w, up_w, down_w):
    width = lax.axis_size("expert")
    rows_dev, routes = experts_hit.shape
    slots = width * CAP
    narrow = tokens.shape[1]
    valid = experts_hit >= 0
    flat = jnp.where(valid, experts_hit * CAP + positions, slots)
    slot_ids = jnp.arange(slots, dtype=jnp.int32)
    hit = flat[None, :, :] == slot_ids[:, None, None]
    onehot = jnp.any(hit, axis=2).astype(jnp.bfloat16)
    slot_gate = jnp.sum(
        jnp.where(hit, gates.astype(jnp.float32)[None, :, :], 0.0), axis=(1, 2)
    ).astype(jnp.bfloat16)
    packed_x = jnp.dot(onehot, tokens, preferred_element_type=jnp.float32).astype(jnp.bfloat16)
    packed_dy = jnp.dot(onehot, cotangent, preferred_element_type=jnp.float32).astype(jnp.bfloat16)
    gate_row = jnp.pad(slot_gate.reshape(width, 1, CAP), ((0, 0), (0, 0), (0, narrow - CAP)))
    block = jnp.concatenate(
        [
            packed_x.reshape(width, CAP, narrow),
            gate_row,
            packed_dy.reshape(width, CAP, narrow),
            jnp.zeros_like(gate_row),
        ],
        axis=1,
    )
    rows_blk = block.shape[1]
    recv = lax.all_to_all(
        block.reshape(width, rows_blk * narrow), "expert", split_axis=0, concat_axis=0, tiled=True
    ).reshape(width, rows_blk, narrow)
    recv_gate = recv[:, CAP, :CAP].reshape(slots)
    pair = jnp.stack(
        [
            recv[:, :CAP, :].reshape(slots, narrow),
            recv[:, CAP + 1 : 2 * CAP + 1, :].reshape(slots, narrow),
        ],
        axis=0,
    )
    full = lax.all_gather(pair, "etp", axis=2, tiled=True)
    stack = jnp.stack([gate_w[0].T, up_w[0].T, down_w[0]], axis=0)
    d_part_b, hidden_b = expert_kernel(lax.axis_index("dp"), full, recv_gate, pieces_dp(stack))
    summed = lax.psum_scatter(d_part_b, "etp", scatter_dimension=1, tiled=True)
    scaled = (recv_gate.astype(jnp.float32)[:, None] * full[1].astype(jnp.float32)).astype(
        jnp.bfloat16
    )
    term = lax.dot_general(
        hidden_b, scaled, (((0,), (0,)), ((), ())), preferred_element_type=jnp.float32
    )
    down_grad = scatter_sum_dp(term.astype(jnp.bfloat16))[None]
    returned = lax.all_to_all(
        summed.reshape(width, CAP * narrow), "expert", split_axis=0, concat_axis=0, tiled=True
    ).reshape(slots, narrow)
    total = lax.dot_general(
        onehot, returned, (((0,), (0,)), ((), ())), preferred_element_type=jnp.float32
    )
    input_grad = total.astype(jnp.bfloat16)
    return (input_grad, down_grad)


def solution(mesh):
    placed = (
        P(("dp", "expert"), "etp"),
        P(("dp", "expert"), "etp"),
        P(("dp", "expert"), None),
        P(("dp", "expert"), None),
        P(("dp", "expert"), None),
        P("expert", "dp", "etp"),
        P("expert", "dp", "etp"),
        P("expert", "etp", "dp"),
    )
    return jax.shard_map(
        local,
        mesh=mesh,
        in_specs=placed,
        out_specs=(P(("dp", "expert"), "etp"), P("expert", "etp", "dp")),
        check_vma=False,
    )
```

```python
import jax
import jax.numpy as jnp
from jax import lax
from jax.experimental import pallas as pl
from jax.experimental.pallas import tpu as pltpu
from jax.sharding import PartitionSpec as P

CAP = 19


def _expert_kernel(me_ref, rows_ref, gate_ref, *refs):
    size = len(refs) - 2
    w_refs = refs[:size]
    q_ref, hidden_ref = refs[size:]
    quarter = w_refs[0].shape[2]
    me = me_ref[0]
    nt = (((1,), (1,)), ((), ()))
    gate_pre = None
    for k in range(size):
        start = pl.multiple_of(((me + size - k) % size) * quarter, quarter)
        f_k = rows_ref[0, :, pl.ds(start, quarter)]
        g_k = rows_ref[1, :, pl.ds(start, quarter)]
        a = lax.dot_general(f_k, w_refs[k][0], nt, preferred_element_type=jnp.float32)
        b = lax.dot_general(f_k, w_refs[k][1], nt, preferred_element_type=jnp.float32)
        c = lax.dot_general(g_k, w_refs[k][2], nt, preferred_element_type=jnp.float32)
        if gate_pre is None:
            gate_pre, up_pre, back = a, b, c
        else:
            gate_pre, up_pre, back = gate_pre + a, up_pre + b, back + c
    sig = jax.nn.sigmoid(gate_pre)
    act = gate_pre * sig
    hidden = act * up_pre
    gate_f = gate_ref[...].astype(jnp.float32)
    d_hidden = gate_f * back
    d_gate_b = (d_hidden * up_pre * sig * (1.0 + gate_pre * (1.0 - sig))).astype(jnp.bfloat16)
    d_up_b = (d_hidden * act).astype(jnp.bfloat16)
    for k in range(size):
        start = pl.multiple_of(((me + size - k) % size) * quarter, quarter)
        part = jnp.dot(d_gate_b, w_refs[k][0], preferred_element_type=jnp.float32)
        part = part + jnp.dot(d_up_b, w_refs[k][1], preferred_element_type=jnp.float32)
        q_ref[:, pl.ds(start, quarter)] = part.astype(jnp.bfloat16)
    hidden_ref[...] = hidden.astype(jnp.bfloat16)


def expert_kernel(me, rows, gate_col, pieces):
    _, slots, width = rows.shape
    ffb = pieces[0].shape[1]
    vmem = pltpu.VMEM
    return pl.pallas_call(
        _expert_kernel,
        out_shape=(
            jax.ShapeDtypeStruct((slots, width), jnp.bfloat16),
            jax.ShapeDtypeStruct((slots, ffb), jnp.bfloat16),
        ),
        in_specs=[pl.BlockSpec(memory_space=pltpu.SMEM)]
        + [pl.BlockSpec(memory_space=vmem)] * (2 + len(pieces)),
        out_specs=(pl.BlockSpec(memory_space=vmem), pl.BlockSpec(memory_space=vmem)),
        compiler_params=pltpu.CompilerParams(vmem_limit_bytes=48 * 1024 * 1024),
    )(me.reshape(1), rows, gate_col.reshape(slots, 1), *pieces)


def pieces_dp(piece):
    size = lax.axis_size("dp")
    got = [piece]
    for shift in range(1, size):
        got.append(lax.ppermute(piece, "dp", [(i, (i + shift) % size) for i in range(size)]))
    return got


def scatter_sum_dp(term_b):
    size = lax.axis_size("dp")
    me = lax.axis_index("dp")
    quarter = term_b.shape[1] // size
    parts = term_b.reshape(term_b.shape[0], size, quarter)
    total = jnp.take(parts, me, axis=1).astype(jnp.float32)
    for shift in range(1, size):
        outgoing = jnp.take(parts, (me + shift) % size, axis=1)
        total = total + lax.ppermute(
            outgoing, "dp", [(i, (i + shift) % size) for i in range(size)]
        ).astype(jnp.float32)
    return total.astype(jnp.bfloat16)


def local(tokens, cotangent, gates, experts_hit, positions, gate_w, up_w, down_w):
    width = lax.axis_size("expert")
    rows_dev, routes = experts_hit.shape
    slots = width * CAP
    narrow = tokens.shape[1]
    valid = experts_hit >= 0
    flat = jnp.where(valid, experts_hit * CAP + positions, slots)
    slot_ids = jnp.arange(slots, dtype=jnp.int32)
    hit = flat[None, :, :] == slot_ids[:, None, None]
    onehot = jnp.any(hit, axis=2).astype(jnp.bfloat16)
    slot_gate = jnp.sum(
        jnp.where(hit, gates.astype(jnp.float32)[None, :, :], 0.0), axis=(1, 2)
    ).astype(jnp.bfloat16)
    packed_x = jnp.dot(onehot, tokens, preferred_element_type=jnp.float32).astype(jnp.bfloat16)
    packed_dy = jnp.dot(onehot, cotangent, preferred_element_type=jnp.float32).astype(jnp.bfloat16)
    gate_row = jnp.pad(slot_gate.reshape(width, 1, CAP), ((0, 0), (0, 0), (0, narrow - CAP)))
    block = jnp.concatenate(
        [
            packed_x.reshape(width, CAP, narrow),
            gate_row,
            packed_dy.reshape(width, CAP, narrow),
            jnp.zeros_like(gate_row),
        ],
        axis=1,
    )
    recv = lax.all_to_all(block, "expert", split_axis=0, concat_axis=0, tiled=True)
    recv_gate = recv[:, CAP, :CAP].reshape(slots)
    pair = jnp.stack(
        [
            recv[:, :CAP, :].reshape(slots, narrow),
            recv[:, CAP + 1 : 2 * CAP + 1, :].reshape(slots, narrow),
        ],
        axis=0,
    )
    full = lax.all_gather(pair, "etp", axis=2, tiled=True)
    stack = jnp.stack([gate_w[0].T, up_w[0].T, down_w[0]], axis=0)
    d_part_b, hidden_b = expert_kernel(lax.axis_index("dp"), full, recv_gate, pieces_dp(stack))
    summed = lax.psum_scatter(d_part_b, "etp", scatter_dimension=1, tiled=True)
    scaled = (recv_gate.astype(jnp.float32)[:, None] * full[1].astype(jnp.float32)).astype(
        jnp.bfloat16
    )
    term = lax.dot_general(
        hidden_b, scaled, (((0,), (0,)), ((), ())), preferred_element_type=jnp.float32
    )
    down_grad = scatter_sum_dp(term.astype(jnp.bfloat16))[None]
    returned = lax.all_to_all(
        summed.reshape(width, 16, CAP * narrow // 16), "expert", split_axis=0, concat_axis=0, tiled=True
    ).reshape(slots, narrow)
    total = lax.dot_general(
        onehot, returned, (((0,), (0,)), ((), ())), preferred_element_type=jnp.float32
    )
    input_grad = total.astype(jnp.bfloat16)
    return (input_grad, down_grad)


def solution(mesh):
    placed = (
        P(("dp", "expert"), "etp"),
        P(("dp", "expert"), "etp"),
        P(("dp", "expert"), None),
        P(("dp", "expert"), None),
        P(("dp", "expert"), None),
        P("expert", "dp", "etp"),
        P("expert", "dp", "etp"),
        P("expert", "etp", "dp"),
    )
    return jax.shard_map(
        local,
        mesh=mesh,
        in_specs=placed,
        out_specs=(P(("dp", "expert"), "etp"), P("expert", "etp", "dp")),
        check_vma=False,
    )
```

```python
import jax
import jax.numpy as jnp
from jax import lax
from jax.experimental import pallas as pl
from jax.experimental.pallas import tpu as pltpu
from jax.sharding import PartitionSpec as P

CAP = 19


def _expert_kernel(me_ref, rows_ref, gate_ref, *refs):
    size = len(refs) - 2
    w_refs = refs[:size]
    q_ref, hidden_ref = refs[size:]
    quarter = w_refs[0].shape[2]
    me = me_ref[0]
    nt = (((1,), (1,)), ((), ()))
    gate_pre = None
    for k in range(size):
        start = pl.multiple_of(((me + size - k) % size) * quarter, quarter)
        f_k = rows_ref[0, :, pl.ds(start, quarter)]
        g_k = rows_ref[1, :, pl.ds(start, quarter)]
        a = lax.dot_general(f_k, w_refs[k][0], nt, preferred_element_type=jnp.float32)
        b = lax.dot_general(f_k, w_refs[k][1], nt, preferred_element_type=jnp.float32)
        c = lax.dot_general(g_k, w_refs[k][2], nt, preferred_element_type=jnp.float32)
        if gate_pre is None:
            gate_pre, up_pre, back = a, b, c
        else:
            gate_pre, up_pre, back = gate_pre + a, up_pre + b, back + c
    sig = jax.nn.sigmoid(gate_pre)
    act = gate_pre * sig
    hidden = act * up_pre
    gate_f = gate_ref[...].astype(jnp.float32)
    d_hidden = gate_f * back
    d_gate_b = (d_hidden * up_pre * sig * (1.0 + gate_pre * (1.0 - sig))).astype(jnp.bfloat16)
    d_up_b = (d_hidden * act).astype(jnp.bfloat16)
    for k in range(size):
        start = pl.multiple_of(((me + size - k) % size) * quarter, quarter)
        part = jnp.dot(d_gate_b, w_refs[k][0], preferred_element_type=jnp.float32)
        part = part + jnp.dot(d_up_b, w_refs[k][1], preferred_element_type=jnp.float32)
        q_ref[:, pl.ds(start, quarter)] = part.astype(jnp.bfloat16)
    hidden_ref[...] = hidden.astype(jnp.bfloat16)


def expert_kernel(me, rows, gate_col, pieces):
    _, slots, width = rows.shape
    ffb = pieces[0].shape[1]
    vmem = pltpu.VMEM
    return pl.pallas_call(
        _expert_kernel,
        out_shape=(
            jax.ShapeDtypeStruct((slots, width), jnp.bfloat16),
            jax.ShapeDtypeStruct((slots, ffb), jnp.bfloat16),
        ),
        in_specs=[pl.BlockSpec(memory_space=pltpu.SMEM)]
        + [pl.BlockSpec(memory_space=vmem)] * (2 + len(pieces)),
        out_specs=(pl.BlockSpec(memory_space=vmem), pl.BlockSpec(memory_space=vmem)),
        compiler_params=pltpu.CompilerParams(vmem_limit_bytes=48 * 1024 * 1024),
    )(me.reshape(1), rows, gate_col.reshape(slots, 1), *pieces)


def pieces_dp(piece):
    size = lax.axis_size("dp")
    got = [piece]
    for shift in range(1, size):
        got.append(lax.ppermute(piece, "dp", [(i, (i + shift) % size) for i in range(size)]))
    return got


def scatter_sum_dp(term_b):
    size = lax.axis_size("dp")
    me = lax.axis_index("dp")
    quarter = term_b.shape[1] // size
    parts = term_b.reshape(term_b.shape[0], size, quarter)
    total = jnp.take(parts, me, axis=1).astype(jnp.float32)
    for shift in range(1, size):
        outgoing = jnp.take(parts, (me + shift) % size, axis=1)
        total = total + lax.ppermute(
            outgoing, "dp", [(i, (i + shift) % size) for i in range(size)]
        ).astype(jnp.float32)
    return total.astype(jnp.bfloat16)


def local(tokens, cotangent, gates, experts_hit, positions, gate_w, up_w, down_w):
    width = lax.axis_size("expert")
    rows_dev, routes = experts_hit.shape
    slots = width * CAP
    narrow = tokens.shape[1]
    valid = experts_hit >= 0
    flat = jnp.where(valid, experts_hit * CAP + positions, slots)
    slot_ids = jnp.arange(slots, dtype=jnp.int32)
    hit = flat[None, :, :] == slot_ids[:, None, None]
    onehot = jnp.any(hit, axis=2).astype(jnp.bfloat16)
    slot_gate = jnp.sum(
        jnp.where(hit, gates.astype(jnp.float32)[None, :, :], 0.0), axis=(1, 2)
    ).astype(jnp.bfloat16)
    packed_x = jnp.dot(onehot, tokens, preferred_element_type=jnp.float32).astype(jnp.bfloat16)
    packed_dy = jnp.dot(onehot, cotangent, preferred_element_type=jnp.float32).astype(jnp.bfloat16)
    gate_row = jnp.pad(slot_gate.reshape(width, 1, CAP), ((0, 0), (0, 0), (0, narrow - CAP)))
    block = jnp.concatenate(
        [
            packed_x.reshape(width, CAP, narrow),
            gate_row,
            packed_dy.reshape(width, CAP, narrow),
            jnp.zeros_like(gate_row),
        ],
        axis=1,
    )
    recv = lax.all_to_all(
        block.reshape(width, 16, -1), "expert", split_axis=0, concat_axis=0, tiled=True
    ).reshape(block.shape)
    recv_gate = recv[:, CAP, :CAP].reshape(slots)
    pair = jnp.stack(
        [
            recv[:, :CAP, :].reshape(slots, narrow),
            recv[:, CAP + 1 : 2 * CAP + 1, :].reshape(slots, narrow),
        ],
        axis=0,
    )
    full = lax.all_gather(pair, "etp", axis=2, tiled=True)
    stack = jnp.stack([gate_w[0].T, up_w[0].T, down_w[0]], axis=0)
    d_part_b, hidden_b = expert_kernel(lax.axis_index("dp"), full, recv_gate, pieces_dp(stack))
    summed = lax.psum_scatter(d_part_b, "etp", scatter_dimension=1, tiled=True)
    scaled = (recv_gate.astype(jnp.float32)[:, None] * full[1].astype(jnp.float32)).astype(
        jnp.bfloat16
    )
    term = lax.dot_general(
        hidden_b, scaled, (((0,), (0,)), ((), ())), preferred_element_type=jnp.float32
    )
    down_grad = scatter_sum_dp(term.astype(jnp.bfloat16))[None]
    returned = lax.all_to_all(
        summed.reshape(width, CAP, narrow), "expert", split_axis=0, concat_axis=0, tiled=True
    ).reshape(slots, narrow)
    total = lax.dot_general(
        onehot, returned, (((0,), (0,)), ((), ())), preferred_element_type=jnp.float32
    )
    input_grad = total.astype(jnp.bfloat16)
    return (input_grad, down_grad)


def solution(mesh):
    placed = (
        P(("dp", "expert"), "etp"),
        P(("dp", "expert"), "etp"),
        P(("dp", "expert"), None),
        P(("dp", "expert"), None),
        P(("dp", "expert"), None),
        P("expert", "dp", "etp"),
        P("expert", "dp", "etp"),
        P("expert", "etp", "dp"),
    )
    return jax.shard_map(
        local,
        mesh=mesh,
        in_specs=placed,
        out_specs=(P(("dp", "expert"), "etp"), P("expert", "etp", "dp")),
        check_vma=False,
    )
```
